256 devices in a mesh: band: 32 (over z, x), wgrp: 8 (over y, core).
Axes of the slice: x: 4, y: 4, z: 8, core: 2. Of those that a mesh axis runs over, the one named last changes fastest.
Arguments:
- visibilities: bfloat16 [8, 2048, 512], P('wgrp', 'band'), may hold values from -6 to 6
- coordinates: bfloat16 [8, 2048, 512], P('wgrp', 'band'), may hold values from -16 to 16
- block_index: int32 [8, 8192], P('wgrp', 'band'), may hold values from 0 to 63
- counts: int32 [8, 1024], P('wgrp', 'band'), may hold values from 1 to 8, as said below
- col_offset: int32 [8, 8192], P('wgrp', 'band'), may hold values from 0 to 8160
Outputs:
- image_rows: float32 [8, 2, 1024, 8192], P('wgrp', None, 'band')
The draws below stay inside these ranges and needn't reach their ends.
Inputs may be any that keep to these rules, and one draw needn't show every extreme that they name: Entry d of a device's row counts the live slots of its list for band d; every device's entry for band 32 // 2 is exactly 8. `block_index`: slots past a list's count read a block too; their subgrids are zero. `col_offset`: A subgrid lies inside its band's rows and the grid's columns.
All inputs are finite; a program needn't handle non-finite values.
Results may differ from the reference program's by a relative error of at most 0.0036.
Values may be sent and summed in bfloat16 or wider, within the bound.
A program may use at most 128 MiB of HBM per device.

```python
import math
import jax
import jax.numpy as jnp
from jax import lax

S = 32
G = 8192
K = 256
NBLK = 64
CAP = 8
NW = 8
N_BAND = 32
N_WGRP = 8


def draw_counts(key, part):
    values = jax.random.randint(key, (N_WGRP, N_BAND * N_BAND), 1, CAP + 1)
    column = jnp.arange(N_BAND * N_BAND) % N_BAND
    return jnp.where(column[None, :] == N_BAND // 2, CAP, values).astype(jnp.int32)


def touch_ends(result, rng, smallest, largest):
    longest = result.shape.index(max(result.shape))
    spots = []
    for shift in (0, 1):
        where = [jax.random.randint(jax.random.fold_in(rng, axis), (), 0, length) for axis, length in enumerate(result.shape)]
        where[longest] = (where[longest] + shift) % result.shape[longest]
        spots.append(tuple(where))
    return result.at[spots[0]].set(smallest).at[spots[1]].set(largest)


def steps_of(key, extent, shards, least, high):
    def one(dim, blocks):
        steps = jax.random.uniform(jax.random.fold_in(jax.random.fold_in(key, 6), dim), (blocks,), jnp.float32, least / len(shards), high / len(shards))
        return jnp.repeat(jnp.exp(steps), extent[dim] // blocks).reshape((-1,) + (1,) * (len(extent) - dim - 1))

    level = one(*shards[0])
    for cut in shards[1:]:
        level = level * one(*cut)
    return level


def noise(own_key, shape, spread, limit, split=(), kind=jnp.bfloat16):
    drawn = jax.random.normal(own_key, shape, jnp.float32) * spread
    if len(split) > 0:
        drawn = steps_of(own_key, shape, split, -0.22, 0.18) * drawn
    return jnp.clip(drawn, min=-limit, max=limit).astype(kind)


def setup_inputs(seed: int = 0) -> dict:
    keys = jax.random.split(jax.random.key(seed), 6)
    visibilities = noise(keys[0], (NW, N_BAND * NBLK, 2 * K), 1.0, 6.0, ((0, 8), (1, 32)))
    coordinates = jnp.clip(jax.random.uniform(keys[1], (NW, N_BAND * NBLK, 2 * K), jnp.float32, -16.0, 16.0) * steps_of(keys[1], (NW, N_BAND * NBLK, 2 * K), ((0, 8), (1, 32)), -0.4, 0.0), -16.0, 16.0).astype(jnp.bfloat16)
    block_index = touch_ends(jax.random.randint(keys[2], (NW, N_BAND * N_BAND * CAP), 0, NBLK), jax.random.fold_in(keys[2], 1), 0, NBLK - 1).astype(jnp.int32)
    counts = draw_counts(jax.random.fold_in(keys[5], 71), 0)
    col_offset = touch_ends(jax.random.randint(keys[4], (NW, N_BAND * N_BAND * CAP), 0, G - S + 1), jax.random.fold_in(keys[4], 1), 0, G - S).astype(jnp.int32)
    return dict(visibilities=visibilities, coordinates=coordinates, block_index=block_index, counts=counts, col_offset=col_offset)


TWO_PI = 2.0 * math.pi

def phase_tables(coord_rows):
    samples = coord_rows.shape[1] // 2
    pixel_pos = (jnp.arange(S, dtype=jnp.float32) - S / 2.0) * (TWO_PI / S)
    coords = coord_rows.astype(jnp.float32)
    angle_x = coords[:, None, :samples] * pixel_pos[None, :, None]
    angle_y = coords[:, None, samples:] * pixel_pos[None, :, None]
    return (angle_x, angle_y)

def weighted_rows(vis_rows, angle_x, angle_y):
    samples = vis_rows.shape[1] // 2
    vis_re = vis_rows[:, None, :samples].astype(jnp.float32)
    vis_im = vis_rows[:, None, samples:].astype(jnp.float32)
    cos_x = jnp.cos(angle_x)
    sin_x = jnp.sin(angle_x)
    weighted_re = (vis_re * cos_x - vis_im * sin_x).astype(jnp.bfloat16)
    weighted_im = (vis_re * sin_x + vis_im * cos_x).astype(jnp.bfloat16)
    cos_y = jnp.cos(angle_y).astype(jnp.bfloat16)
    sin_y = jnp.sin(angle_y).astype(jnp.bfloat16)
    return (weighted_re, weighted_im, cos_y, sin_y)

def product(left, right):
    return jnp.einsum('nyk,nxk->nyx', left.astype(jnp.float32), right.astype(jnp.float32))

def make_subgrids(vis_rows, coord_rows):
    angle_x, angle_y = phase_tables(coord_rows)
    weighted_re, weighted_im, cos_y, sin_y = weighted_rows(vis_rows, angle_x, angle_y)
    sub_re = product(cos_y, weighted_re) - product(sin_y, weighted_im)
    sub_im = product(cos_y, weighted_im) + product(sin_y, weighted_re)
    return jnp.stack([sub_re, sub_im], axis=1)

def reference(visibilities, coordinates, block_index, counts, col_offset):
    slot_total = N_BAND * CAP

    def one_group(arrays):
        vis_group, coord_group, block_group, count_group, offset_group = arrays

        def add_source(slab, source):
            vis_store = lax.dynamic_slice_in_dim(vis_group, source * NBLK, NBLK, 0)
            coord_store = lax.dynamic_slice_in_dim(coord_group, source * NBLK, NBLK, 0)
            blocks = lax.dynamic_slice_in_dim(block_group, source * slot_total, slot_total, 0)
            counts_row = lax.dynamic_slice_in_dim(count_group, source * N_BAND, N_BAND, 0)
            offsets = lax.dynamic_slice_in_dim(offset_group, source * slot_total, slot_total, 0)
            slot_live = (jnp.arange(CAP, dtype=jnp.int32)[None, :] < counts_row[:, None]).reshape(-1)
            chosen_vis = jnp.take(vis_store, blocks, axis=0)
            chosen_coord = jnp.take(coord_store, blocks, axis=0)
            subgrids = make_subgrids(chosen_vis, chosen_coord)
            subgrids = subgrids * slot_live.astype(jnp.float32)[:, None, None, None]
            dest_band = (jnp.arange(slot_total, dtype=jnp.int32) // CAP).astype(jnp.int32)
            pixel_index = jnp.arange(S, dtype=jnp.int32)
            row_index = (dest_band[:, None] * S + pixel_index[None, :]).astype(jnp.int32)
            column_index = (offsets[:, None] + pixel_index[None, :]).astype(jnp.int32)
            slab = slab.at[:, row_index[:, :, None], column_index[:, None, :]].add(jnp.transpose(subgrids, (1, 0, 2, 3)))
            return (slab, None)
        empty_slab = jnp.zeros((2, N_BAND * S, G), jnp.float32)
        slab, unused = lax.scan(add_source, empty_slab, jnp.arange(N_BAND, dtype=jnp.int32))
        return slab
    grid = lax.map(one_group, (visibilities, coordinates, block_index, counts, col_offset))
    norm_scale = 1.0 / math.sqrt(G * K)

    def fold_transform(group_index):
        own_slab = grid[group_index]
        mirror_slab = grid[N_WGRP - 1 - group_index][:, ::-1, ::-1]
        folded_re = own_slab[0] + mirror_slab[0]
        folded_im = own_slab[1] - mirror_slab[1]
        spectrum = jnp.fft.fft(lax.complex(folded_re, folded_im), axis=-1)
        return jnp.stack([jnp.real(spectrum), jnp.imag(spectrum)]) * norm_scale
    return lax.map(fold_transform, jnp.arange(N_WGRP, dtype=jnp.int32))
```

```python
import functools
import math

import jax
import jax.numpy as jnp
import numpy as np
from jax import lax
from jax.experimental import pallas as pl
from jax.experimental.pallas import tpu as pltpu
from jax.sharding import PartitionSpec as P

S = 32
G = 8192
K = 256
CAP = 8
NBLK = 64
LANES = 128
TILES = G // LANES
HALF = S // 2
MESH = pl.DeviceIdType.MESH
F32 = jnp.float32
BF16 = jnp.bfloat16


def fit(func, degree):
    nodes = 0.125 + 0.125 * np.cos(np.pi * (np.arange(400) + 0.5) / 400)
    series = np.polynomial.chebyshev.Chebyshev.fit(nodes, func(nodes), degree, domain=[0, 0.25])
    return [float(c) for c in series.convert(kind=np.polynomial.Polynomial).coef]


SIN_COEF = fit(lambda q: np.sin(2 * np.pi * np.sqrt(q)) / np.sqrt(q), 6)
COS_COEF = fit(lambda q: np.cos(2 * np.pi * np.sqrt(q)), 7)


def horner(coef, q):
    total = jnp.full_like(q, coef[-1])
    for c in coef[-2::-1]:
        total = total * q + c
    return total


def unit(cycles):
    frac = cycles - jnp.floor(cycles + 0.5)
    q = frac * frac
    return horner(COS_COEF, q), frac * horner(SIN_COEF, q)


def cmul(a, b):
    return a[0] * b[0] - a[1] * b[1], a[0] * b[1] + a[1] * b[0]


def subgrid_kernel(index_ref, counts_ref, vis_ref, coord_ref, out_ref, vf_ref, cf_ref, z_ref, sub_ref):
    vf_ref[...] = vis_ref[...].astype(F32)
    cf_ref[...] = coord_ref[...].astype(F32)
    for axis in range(2):
        pos = cf_ref[:, axis * K : (axis + 1) * K]
        for which, step in enumerate((1.0, 8.0, 16.0)):
            re, im = unit(pos * (step / S))
            z_ref[axis, which, 0] = re
            z_ref[axis, which, 1] = im
    eighth = lax.broadcasted_iota(jnp.int32, (8, K), 0).astype(F32) * (1.0 / S)
    sub_ref[:, NBLK] = jnp.zeros((2, S, LANES), BF16)

    def one_block(m):
        row = pl.ds(m, 1)

        def powers(axis, which):
            return z_ref[axis, which, 0, row, :], z_ref[axis, which, 1, row, :]

        base = unit(cf_ref[row, 0:K] * eighth)
        z8 = powers(0, 1)
        z16 = powers(0, 2)
        rr, ii, ri, ir = z8[0] * base[0], z8[1] * base[1], z8[0] * base[1], z8[1] * base[0]
        low = (z16[0] * base[0] + z16[1] * base[1], z16[0] * base[1] - z16[1] * base[0])
        parts = (low, (rr + ii, ri - ir), base, (rr - ii, ri + ir))
        vis = (vf_ref[row, 0:K], vf_ref[row, K : 2 * K])
        mirrored = cmul((vis[0], -vis[1]), powers(0, 0))
        weights = []
        for factor in (vis, mirrored):
            made = [cmul(factor, part) for part in parts]
            weights.append(
                jnp.concatenate(
                    [jnp.concatenate([c[0] for c in made], 0), jnp.concatenate([c[1] for c in made], 0)], 1
                ).astype(BF16)
            )
        base = unit(cf_ref[row, K : 2 * K] * eighth)
        z8 = powers(1, 1)
        z16 = powers(1, 2)
        pair = (
            cmul((z16[0], -z16[1]), base),
            cmul((z8[0], -z8[1]), base),
        )
        table = (jnp.concatenate([pair[0][0], pair[1][0]], 0), jnp.concatenate([pair[0][1], pair[1][1]], 0))
        rows = []
        for cos, sin in (table, cmul(powers(1, 0), table)):
            rows.append(jnp.concatenate([cos, -sin], 1))
            rows.append(jnp.concatenate([sin, cos], 1))
        left = jnp.concatenate(rows, 0).astype(BF16)
        right = jnp.concatenate(weights, 0)
        made = lax.dot_general(left, right, (((1,), (1,)), ((), ())), preferred_element_type=F32)
        for half in range(2):
            piece = made[half * S : (half + 1) * S, half * S : (half + 1) * S]
            sub_ref[half, m] = jnp.concatenate([piece] * 4, 1).astype(BF16)

    def some_blocks(i, carry):
        for j in range(2):
            one_block(i * 2 + j)
        return carry

    lax.fori_loop(0, NBLK // 2, some_blocks, 0)
    lane = lax.broadcasted_iota(jnp.int32, (S, LANES), 1) // S

    def expand(d, carry):
        live = counts_ref[0, d]
        for group in range(2):
            idx = []
            for j in range(4):
                slot = group * 4 + j
                idx.append(jnp.where(slot < live, index_ref[0, d * CAP + slot], NBLK))
            for half in range(2):
                value = sub_ref[half, idx[3]]
                for j in range(3):
                    value = jnp.where(lane == j, sub_ref[half, idx[j]], value)
                out_ref[half, d, group] = value
        return carry

    lax.fori_loop(0, S, expand, 0)


def make_subgrids(vis, coord, index, counts):
    vmem = pl.BlockSpec(memory_space=pltpu.VMEM)
    smem = pl.BlockSpec(memory_space=pltpu.SMEM)
    return pl.pallas_call(
        subgrid_kernel,
        out_shape=jax.ShapeDtypeStruct((2, S, 2, S, LANES), BF16),
        in_specs=[smem, smem, vmem, vmem],
        out_specs=vmem,
        scratch_shapes=[
            pltpu.VMEM((NBLK, 2 * K), F32),
            pltpu.VMEM((NBLK, 2 * K), F32),
            pltpu.VMEM((2, 3, 2, NBLK, K), F32),
            pltpu.VMEM((2, NBLK + 1, S, LANES), BF16),
        ],
        name="subgrids",
    )(index, counts, vis, coord)


def exchange_kernel(send_ref, offs_ref, recv_ref, roff_ref, send_sem, recv_sem, osend_sem, orecv_sem, own_sem):
    band = lax.axis_index("band")
    plane = lax.axis_index("wgrp")
    z = band // 4
    x = band % 4

    def peer(j):
        turn = j // 8
        dz = 4 + ((turn + 1) // 2) * (2 * (turn % 2) - 1)
        dx = 3 - (j // 2) % 4
        half = 1 - j % 2
        return half, ((z + dz) % 8) * 4 + (x + dx) % 4

    def device(half, d):
        return (d + half * (31 - 2 * d), plane + half * (7 - 2 * plane))

    barrier = pltpu.get_barrier_semaphore()

    def greet(j, carry):
        half, d = peer(j)
        pl.semaphore_signal(barrier, inc=1, device_id=device(half, d), device_id_type=MESH)
        return carry

    lax.fori_loop(0, 63, greet, 0)
    own = pltpu.make_async_copy(send_ref.at[0, band], recv_ref.at[0, band], own_sem.at[0])
    own.start()
    own_offs = pltpu.make_async_copy(offs_ref.at[0, band], roff_ref.at[0, band], own_sem.at[1])
    own_offs.start()
    pl.semaphore_wait(barrier, 63)

    def copies(j):
        half, d = peer(j)
        data = pltpu.make_async_remote_copy(
            src_ref=send_ref.at[half, d],
            dst_ref=recv_ref.at[half, band],
            send_sem=send_sem.at[half, d],
            recv_sem=recv_sem.at[half, band],
            device_id=device(half, d),
            device_id_type=MESH,
        )
        offs = pltpu.make_async_remote_copy(
            src_ref=offs_ref.at[half, d],
            dst_ref=roff_ref.at[half, band],
            send_sem=osend_sem.at[half, d],
            recv_sem=orecv_sem.at[half, band],
            device_id=device(half, d),
            device_id_type=MESH,
        )
        return data, offs

    def start(j, carry):
        data, offs = copies(j)
        data.start()
        offs.start()
        return carry

    lax.fori_loop(0, 63, start, 0)
    own.wait()
    own_offs.wait()

    def finish(j, carry):
        half, d = peer(j)
        data, offs = copies(j)
        data.wait_send()
        offs.wait_send()
        for dst, sem, src in ((recv_ref, recv_sem, send_ref), (roff_ref, orecv_sem, offs_ref)):
            pltpu.make_async_remote_copy(
                src_ref=src.at[half, d],
                dst_ref=dst.at[half, d],
                send_sem=send_sem.at[half, d],
                recv_sem=sem.at[half, d],
                device_id=device(half, d),
                device_id_type=MESH,
            ).wait_recv()
        return carry

    lax.fori_loop(0, 63, finish, 0)


def exchange(lists, offsets):
    anywhere = pl.BlockSpec(memory_space=pl.ANY)
    return pl.pallas_call(
        exchange_kernel,
        out_shape=(
            jax.ShapeDtypeStruct(lists.shape, lists.dtype),
            jax.ShapeDtypeStruct(offsets.shape, offsets.dtype),
        ),
        in_specs=[anywhere, anywhere],
        out_specs=(anywhere, anywhere),
        scratch_shapes=[pltpu.SemaphoreType.DMA((2, S))] * 4 + [pltpu.SemaphoreType.DMA((2,))],
        compiler_params=pltpu.CompilerParams(collective_id=0, has_side_effects=True),
        name="exchange",
    )(lists, offsets)


def place_kernel(offs_ref, lists_ref, out_ref, low_ref, *slabs):
    zero = jnp.zeros((S, LANES), F32)

    def clear(t, carry):
        for slab in slabs:
            slab[t] = zero
        return carry

    lax.fori_loop(0, TILES + 1, clear, 0)
    lane = lax.broadcasted_iota(jnp.int32, (S, LANES), 1)

    def place(i, carry):
        half = i // (2 * S)
        source = (i // 2) % S
        group = i % 2
        values = lists_ref[half, source, group].astype(F32)
        for j, slab in enumerate(slabs):
            start = offs_ref[half, source, 0, group * 4 + j]
            tile = start // LANES
            first = start % LANES
            turned = pltpu.roll(values, (first + LANES - S * j) % LANES, 1)
            slab[tile] += jnp.where((lane >= first) & (lane < first + S), turned, zero)
            slab[tile + 1] += jnp.where(lane < first + S - LANES, turned, zero)
        return carry

    lax.fori_loop(0, 4 * S, place, 0, unroll=2)

    def gather(t, carry):
        total = (slabs[0][t] + slabs[1][t]) + (slabs[2][t] + slabs[3][t])
        out_ref[t] = total
        low_ref[t] = total.astype(BF16)
        return carry

    lax.fori_loop(0, TILES, gather, 0)


def place(offsets, lists):
    vmem = pl.BlockSpec(memory_space=pltpu.VMEM)
    return pl.pallas_call(
        place_kernel,
        out_shape=(
            jax.ShapeDtypeStruct((TILES, S, LANES), F32),
            jax.ShapeDtypeStruct((TILES, S, LANES), BF16),
        ),
        in_specs=[pl.BlockSpec(memory_space=pltpu.SMEM), vmem],
        out_specs=(vmem, vmem),
        scratch_shapes=[pltpu.VMEM((TILES + 1, S, LANES), F32)] * 4,
        name="place",
    )(offsets, lists)


def fft8(values):
    half = math.sqrt(0.5)

    def add(a, b):
        return a[0] + b[0], a[1] + b[1]

    def sub(a, b):
        return a[0] - b[0], a[1] - b[1]

    def turn(a):
        return a[1], -a[0]

    def fft4(v):
        s0, d0 = add(v[0], v[2]), sub(v[0], v[2])
        s1, d1 = add(v[1], v[3]), turn(sub(v[1], v[3]))
        return add(s0, s1), add(d0, d1), sub(s0, s1), sub(d0, d1)

    even = fft4(values[0::2])
    odd = fft4(values[1::2])
    o1 = ((odd[1][0] + odd[1][1]) * half, (odd[1][1] - odd[1][0]) * half)
    o2 = turn(odd[2])
    o3 = ((odd[3][1] - odd[3][0]) * half, (odd[3][0] + odd[3][1]) * -half)
    odd = (odd[0], o1, o2, o3)
    return [add(e, o) for e, o in zip(even, odd)] + [sub(e, o) for e, o in zip(even, odd)]


def transform_kernel(flip, rows_ref, twist_ref, matrix_ref, *rest):
    out_ref, mid_ref, sec_ref = rest[-3:]
    for part in range(2):
        lo, hi = 8 * part, HALF + 8 * part
        for t2 in range(8):
            made = fft8(
                [
                    (
                        rows_ref[8 * t1 + t2, lo : lo + 8, :].astype(F32),
                        rows_ref[8 * t1 + t2, hi : hi + 8, :].astype(F32),
                    )
                    for t1 in range(8)
                ]
            )
            for q1 in range(8):
                re, im = made[q1]
                angle = -2 * math.pi * t2 * q1 / 64
                if t2 * q1:
                    c, s = math.cos(angle), math.sin(angle)
                    re, im = re * c - im * s, im * c + re * s
                mid_ref[0, q1 * 8 + t2] = re
                mid_ref[1, q1 * 8 + t2] = im
        for q1 in range(8):
            made = fft8([(mid_ref[0, q1 * 8 + t2], mid_ref[1, q1 * 8 + t2]) for t2 in range(8)])
            for q2 in range(8):
                at = (q1 + 8 * q2) * 8
                sec_ref[0, part, at : at + 8] = made[q2][0]
                sec_ref[1, part, at : at + 8] = made[q2][1]
    contract = (((1,), (1,)), ((), ()))
    high = matrix_ref[0]
    low = matrix_ref[1]
    for r in range(HALF):
        part, i = r // 8, r % 8
        sr = sec_ref[0, part, pl.ds(i, TILES, stride=8), :]
        si = sec_ref[1, part, pl.ds(i, TILES, stride=8), :]
        zr, zi = [], []
        for k in range(2):
            tr = twist_ref[0, k * TILES : (k + 1) * TILES]
            ti = twist_ref[1, k * TILES : (k + 1) * TILES]
            zr.append(sr * tr - si * ti)
            zi.append(si * tr + sr * ti)
        full = jnp.concatenate([jnp.concatenate(zr, 0), jnp.concatenate(zi, 0)], 1)
        top = full.astype(BF16)
        rest_ = (full - top.astype(F32)).astype(BF16)
        made = (
            lax.dot_general(high, top, contract, preferred_element_type=F32)
            + lax.dot_general(low, top, contract, preferred_element_type=F32)
            + lax.dot_general(high, rest_, contract, preferred_element_type=F32)
        )
        place_at = HALF - 1 - r if flip else r
        part, i = place_at // 8, place_at % 8
        out_ref[0, part, pl.ds(i, TILES, stride=8), :] = made[:TILES]
        out_ref[1, part, pl.ds(i, TILES, stride=8), :] = made[TILES:]


def tables(flip):
    shift = 1 if flip else 0
    k = np.arange(LANES)[:, None]
    n = np.arange(LANES)[None, :] + shift
    angle = -2 * np.pi * ((k * n) % G) / G
    twist = np.stack([np.cos(angle), np.sin(angle)]) / math.sqrt(G * K)
    t = np.arange(TILES)[:, None]
    angle = 2 * np.pi * ((t * n) % TILES) / TILES
    c, s = np.cos(angle), np.sin(angle)
    sign = -1.0 if flip else 1.0
    matrix = np.concatenate([np.concatenate([c, s], 1), sign * np.concatenate([-s, c], 1)], 0)
    high = matrix.astype(BF16)
    low = (matrix - high.astype(np.float64)).astype(BF16)
    return twist.astype(np.float32), np.stack([high, low])


def transform(rows, flip, earlier=None):
    vmem = pl.BlockSpec(memory_space=pltpu.VMEM)
    where = 1 if flip else 0
    args = list(map(jnp.asarray, tables(flip)))
    specs = [vmem, vmem, vmem]
    if earlier is not None:
        args.append(earlier)
        specs.append(pl.BlockSpec(memory_space=pl.ANY))
    return pl.pallas_call(
        functools.partial(transform_kernel, flip),
        grid=(1,),
        out_shape=jax.ShapeDtypeStruct((2, 4, 8 * TILES, LANES), F32),
        in_specs=specs,
        out_specs=pl.BlockSpec((2, 2, 8 * TILES, LANES), lambda i: (0, where, 0, 0)),
        scratch_shapes=[
            pltpu.VMEM((2, TILES, 8, LANES), F32),
            pltpu.VMEM((2, 2, 8 * TILES, LANES), F32),
        ],
        input_output_aliases={} if earlier is None else {3: 0},
        cost_estimate=pl.CostEstimate(flops=600_000_000, bytes_accessed=4_000_000, transcendentals=0),
        name="transform_mirror" if flip else "transform_own",
    )(rows, *args)


def shards(visibilities, coordinates, block_index, counts, col_offset):
    lists = make_subgrids(visibilities[0], coordinates[0], block_index, counts)
    firsts = jnp.stack([col_offset, G - S - col_offset]).reshape(2, S, 1, CAP)
    firsts = jnp.pad(firsts, ((0, 0), (0, 0), (0, 0), (0, LANES - CAP)))
    lists, firsts = exchange(lists, firsts)
    own, low = place(firsts, lists)
    total = lax.axis_size("band") * lax.axis_size("wgrp")
    other = lax.ppermute(low, ("band", "wgrp"), [(i, total - 1 - i) for i in range(total)])
    out = transform(own, False)
    out = transform(other, True, out)
    out = out.reshape(2, 4, TILES, 8, LANES)
    return jnp.transpose(out, (0, 1, 3, 2, 4)).reshape(1, 2, S, G)


def solution(mesh):
    placed = (
        P("wgrp", "band", None),
        P("wgrp", "band", None),
        P("wgrp", "band"),
        P("wgrp", "band"),
        P("wgrp", "band"),
    )
    return jax.shard_map(
        shards, mesh=mesh, in_specs=placed, out_specs=P("wgrp", None, "band", None), check_vma=False
    )
```

```python
import functools
import math

import jax
import jax.numpy as jnp
import numpy as np
from jax import lax
from jax.experimental import pallas as pl
from jax.experimental.pallas import tpu as pltpu
from jax.sharding import PartitionSpec as P

S = 32
G = 8192
K = 256
CAP = 8
NBLK = 64
LANES = 128
TILES = G // LANES
HALF = S // 2
MESH = pl.DeviceIdType.MESH
F32 = jnp.float32
BF16 = jnp.bfloat16


def fit(func, degree):
    nodes = 0.125 + 0.125 * np.cos(np.pi * (np.arange(400) + 0.5) / 400)
    series = np.polynomial.chebyshev.Chebyshev.fit(nodes, func(nodes), degree, domain=[0, 0.25])
    return [float(c) for c in series.convert(kind=np.polynomial.Polynomial).coef]


SIN_COEF = fit(lambda q: np.sin(2 * np.pi * np.sqrt(q)) / np.sqrt(q), 6)
COS_COEF = fit(lambda q: np.cos(2 * np.pi * np.sqrt(q)), 7)


def horner(coef, q):
    total = jnp.full_like(q, coef[-1])
    for c in coef[-2::-1]:
        total = total * q + c
    return total


def unit(cycles):
    frac = cycles - jnp.floor(cycles + 0.5)
    q = frac * frac
    return horner(COS_COEF, q), frac * horner(SIN_COEF, q)


def cmul(a, b):
    return a[0] * b[0] - a[1] * b[1], a[0] * b[1] + a[1] * b[0]


def spread(index_ref, counts_ref, vis_ref, coord_ref, offs_ref, recv_ref, roff_ref, *scratch):
    vf_ref, z_ref, sub_ref, send_ref, send_sem, recv_sem, osend_sem, orecv_sem, own_sem = scratch
    band = lax.axis_index("band")
    plane = lax.axis_index("wgrp")
    z = band // 4
    x = band % 4

    def target(j):
        turn = j // 4
        dz = 4 + ((turn + 1) // 2) * (2 * (turn % 2) - 1)
        dx = 3 - j % 4
        return ((z + dz) % 8) * 4 + (x + dx) % 4

    def device(half, d):
        return (d + half * (31 - 2 * d), plane + half * (7 - 2 * plane))

    barrier = pltpu.get_barrier_semaphore()

    def greet(j, carry):
        pl.semaphore_signal(barrier, inc=1, device_id=device(0, target(j)), device_id_type=MESH)
        pl.semaphore_signal(barrier, inc=1, device_id=device(1, target(j)), device_id_type=MESH)
        return carry

    lax.fori_loop(0, S - 1, greet, 0)
    pl.semaphore_signal(barrier, inc=1, device_id=device(1, band), device_id_type=MESH)

    vf_ref[...] = vis_ref[...].astype(F32)
    for axis in range(2):
        step = unit(coord_ref[:, axis * K : (axis + 1) * K].astype(F32) * (1.0 / S))
        for which in range(5):
            z_ref[axis, which, 0] = step[0]
            z_ref[axis, which, 1] = step[1]
            if which < 4:
                step = ((step[0] - step[1]) * (step[0] + step[1]), 2.0 * (step[0] * step[1]))
    sub_ref[:, NBLK] = jnp.zeros((2, S, LANES), BF16)
    sublane = lax.broadcasted_iota(jnp.int32, (8, K), 0)
    bits = [(sublane & bit) != 0 for bit in (1, 2, 4)]
    first = sublane == 0

    def one_block(m):
        row = pl.ds(m, 1)

        def power(axis, which):
            return z_ref[axis, which, 0, row, :], z_ref[axis, which, 1, row, :]

        def low_powers(axis):
            factors = []
            for which, bit in enumerate(bits):
                re, im = power(axis, which)
                factors.append((jnp.where(bit, re, 1.0), jnp.where(bit, im, 0.0)))
            return cmul(cmul(factors[0], factors[1]), factors[2])

        base = low_powers(0)
        z8 = power(0, 3)
        z16 = power(0, 4)
        rr, ii, ri, ir = z8[0] * base[0], z8[1] * base[1], z8[0] * base[1], z8[1] * base[0]
        low = (z16[0] * base[0] + z16[1] * base[1], z16[0] * base[1] - z16[1] * base[0])
        parts = (low, (rr + ii, ri - ir), base, (rr - ii, ri + ir))
        a, b = vf_ref[row, 0:K], vf_ref[row, K : 2 * K]
        plain, turned = [], []
        for i, (re, im) in enumerate(parts):
            ar, bi, ai, br = a * re, b * im, a * im, b * re
            plain.append((ar - bi, ai + br))
            if i == 0:
                re, im = jnp.where(first, z16[0], re), jnp.where(first, z16[1], im)
                ar, bi, ai, br = a * re, b * im, a * im, b * re
            turned.append((ar + bi, ai - br))
        right = jnp.concatenate(
            [
                jnp.concatenate([jnp.concatenate([c[i] for c in made], 0) for i in range(2)], 1).astype(BF16)
                for made in (plain, turned)
            ],
            0,
        )
        base = low_powers(1)
        z8 = power(1, 3)
        z16 = power(1, 4)
        pair = (cmul((z16[0], -z16[1]), base), cmul((z8[0], -z8[1]), base))
        step = power(1, 0)
        rows = []
        for table in (pair, tuple(cmul(step, p) for p in pair)):
            cos = jnp.concatenate([p[0] for p in table], 0)
            sin = jnp.concatenate([p[1] for p in table], 0)
            rows.append(jnp.concatenate([cos, -sin], 1))
            rows.append(jnp.concatenate([sin, cos], 1))
        left = jnp.concatenate(rows, 0).astype(BF16)
        made = lax.dot_general(left, right, (((1,), (1,)), ((), ())), preferred_element_type=F32)
        for half in range(2):
            piece = made[half * S : (half + 1) * S, half * S : (half + 1) * S]
            piece = jnp.concatenate([piece] * 4, 1)
            if half:
                piece = pltpu.roll(piece, LANES - 1, 1)
            sub_ref[half, m] = piece.astype(BF16)

    def some_blocks(i, carry):
        for j in range(4):
            one_block(i * 4 + j)
        return carry

    lax.fori_loop(0, NBLK // 4, some_blocks, 0)
    lane = lax.broadcasted_iota(jnp.int32, (S, LANES), 1) // S

    def expand(j):
        d = target(j)
        live = counts_ref[0, d]
        for group in range(2):
            idx = []
            for i in range(4):
                slot = group * 4 + i
                idx.append(jnp.where(slot < live, index_ref[0, d * CAP + slot], NBLK))
            for half in range(2):
                value = sub_ref[half, idx[3]]
                for i in range(3):
                    value = jnp.where(lane == i, sub_ref[half, idx[i]], value)
                send_ref[half, d, group] = value

    def copies(half, j):
        d = target(j)
        data = pltpu.make_async_remote_copy(
            src_ref=send_ref.at[half, d],
            dst_ref=recv_ref.at[half, band],
            send_sem=send_sem.at[half],
            recv_sem=recv_sem.at[half],
            device_id=device(half, d),
            device_id_type=MESH,
        )
        offs = pltpu.make_async_remote_copy(
            src_ref=offs_ref.at[d // 16],
            dst_ref=roff_ref.at[half, band],
            send_sem=osend_sem.at[half],
            recv_sem=orecv_sem.at[half],
            device_id=device(half, d),
            device_id_type=MESH,
        )
        return data, offs

    def send(half, j):
        for copy in copies(half, j):
            copy.start()

    expand(0)
    pl.semaphore_wait(barrier, 2 * S - 1)

    def pass_on(j, carry):
        expand(j)
        send(0, j - 1)
        send(1, j - 1)
        return carry

    lax.fori_loop(1, S, pass_on, 0)
    own_offs = pltpu.make_async_copy(offs_ref.at[band // 16], roff_ref.at[0, band], own_sem.at[1])
    own_offs.start()
    send(1, S - 1)
    own = pltpu.make_async_copy(send_ref.at[0, band], recv_ref.at[0, band], own_sem.at[0])
    own.start()
    own_offs.wait()
    own.wait()
    for half, count in ((0, S - 1), (1, S)):
        for arrived, left_sem, come_sem in ((roff_ref, osend_sem, orecv_sem), (recv_ref, send_sem, recv_sem)):
            everything = arrived.at[half, 0:count]
            both = pltpu.make_async_remote_copy(
                src_ref=everything,
                dst_ref=everything,
                send_sem=left_sem.at[half],
                recv_sem=come_sem.at[half],
                device_id=device(1, band),
                device_id_type=MESH,
            )
            both.wait_send()
            both.wait_recv()


def spread_lists(vis, coord, index, counts, offsets):
    anywhere = pl.BlockSpec(memory_space=pl.ANY)
    vmem = pl.BlockSpec(memory_space=pltpu.VMEM)
    smem = pl.BlockSpec(memory_space=pltpu.SMEM)
    return pl.pallas_call(
        spread,
        out_shape=(
            jax.ShapeDtypeStruct((2, S, 2, S, LANES), BF16),
            jax.ShapeDtypeStruct((2, S, 1, LANES), jnp.int32),
        ),
        in_specs=[smem, smem, vmem, vmem, anywhere],
        out_specs=(anywhere, anywhere),
        scratch_shapes=[
            pltpu.VMEM((NBLK, 2 * K), F32),
            pltpu.VMEM((2, 5, 2, NBLK, K), F32),
            pltpu.VMEM((2, NBLK + 1, S, LANES), BF16),
            pltpu.VMEM((2, S, 2, S, LANES), BF16),
        ]
        + [pltpu.SemaphoreType.DMA((2,))] * 5,
        compiler_params=pltpu.CompilerParams(collective_id=0, has_side_effects=True),
        name="spread",
    )(index, counts, vis, coord, offsets)


def place_kernel(offs_ref, lists_ref, out_ref, low_ref, *slabs):
    zero = jnp.zeros((8, LANES), F32)
    band = lax.axis_index("band")

    def clear(t, carry):
        for slab in slabs:
            slab[t] = jnp.zeros((S, LANES), F32)
        return carry

    lax.fori_loop(0, TILES + 1, clear, 0)
    lane = lax.broadcasted_iota(jnp.int32, (8, LANES), 1)

    for half in range(2):
        base = ((31 - band if half else band) & 15) * CAP

        def place(i, carry, half=half, base=base):
            for group in range(2):
                values = lists_ref[half, i, group].astype(F32)
                for j, slab in enumerate(slabs):
                    start = offs_ref[half, i, 0, base + (group * 4 + j)]
                    if half:
                        start = G - S - start
                    tile = lax.shift_right_logical(start, 7)
                    first = start & (LANES - 1)
                    turned = pltpu.roll(values, (first - S * j) & (LANES - 1), 1)
                    inner = (lane >= first) & (lane < first + S)
                    outer = lane < first + (S - LANES)
                    for p in range(0, S, 8):
                        slab[tile, p : p + 8] += jnp.where(inner, turned[p : p + 8], zero)
                        slab[tile + 1, p : p + 8] += jnp.where(outer, turned[p : p + 8], zero)
            return carry

        lax.fori_loop(0, S, place, 0, unroll=4)

    def gather(t, carry):
        total = (slabs[0][t] + slabs[1][t]) + (slabs[2][t] + slabs[3][t])
        out_ref[t] = total
        low_ref[t] = total.astype(BF16)
        return carry

    lax.fori_loop(0, TILES, gather, 0)


def place(offsets, lists):
    vmem = pl.BlockSpec(memory_space=pltpu.VMEM)
    return pl.pallas_call(
        place_kernel,
        out_shape=(
            jax.ShapeDtypeStruct((TILES, S, LANES), F32),
            jax.ShapeDtypeStruct((TILES, S, LANES), BF16),
        ),
        in_specs=[pl.BlockSpec(memory_space=pltpu.SMEM), vmem],
        out_specs=(vmem, vmem),
        scratch_shapes=[pltpu.VMEM((TILES + 1, S, LANES), F32)] * 4,
        name="place",
    )(offsets, lists)


def fft8(values):
    half = math.sqrt(0.5)

    def add(a, b):
        return a[0] + b[0], a[1] + b[1]

    def sub(a, b):
        return a[0] - b[0], a[1] - b[1]

    def turn(a):
        return a[1], -a[0]

    def fft4(v):
        s0, d0 = add(v[0], v[2]), sub(v[0], v[2])
        s1, d1 = add(v[1], v[3]), turn(sub(v[1], v[3]))
        return add(s0, s1), add(d0, d1), sub(s0, s1), sub(d0, d1)

    even = fft4(values[0::2])
    odd = fft4(values[1::2])
    o1 = ((odd[1][0] + odd[1][1]) * half, (odd[1][1] - odd[1][0]) * half)
    o2 = turn(odd[2])
    o3 = ((odd[3][1] - odd[3][0]) * half, (odd[3][0] + odd[3][1]) * -half)
    odd = (odd[0], o1, o2, o3)
    return [add(e, o) for e, o in zip(even, odd)] + [sub(e, o) for e, o in zip(even, odd)]


def transform_kernel(flip, rows_ref, twist_ref, matrix_ref, *rest):
    out_ref, mid_ref, sec_ref = rest[-3:]
    for part in range(2):
        lo, hi = 8 * part, HALF + 8 * part
        for t2 in range(8):
            made = fft8(
                [
                    (
                        rows_ref[8 * t1 + t2, lo : lo + 8, :].astype(F32),
                        rows_ref[8 * t1 + t2, hi : hi + 8, :].astype(F32),
                    )
                    for t1 in range(8)
                ]
            )
            for q1 in range(8):
                re, im = made[q1]
                angle = -2 * math.pi * t2 * q1 / 64
                if t2 * q1:
                    c, s = math.cos(angle), math.sin(angle)
                    re, im = re * c - im * s, im * c + re * s
                mid_ref[0, q1 * 8 + t2] = re
                mid_ref[1, q1 * 8 + t2] = im
        for q1 in range(8):
            made = fft8([(mid_ref[0, q1 * 8 + t2], mid_ref[1, q1 * 8 + t2]) for t2 in range(8)])
            for q2 in range(8):
                at = (q1 + 8 * q2) * 8
                sec_ref[0, part, at : at + 8] = made[q2][0]
                sec_ref[1, part, at : at + 8] = made[q2][1]
    contract = (((1,), (1,)), ((), ()))
    high = matrix_ref[0]
    low = matrix_ref[1]
    for r in range(HALF):
        part, i = r // 8, r % 8
        sr = sec_ref[0, part, pl.ds(i, TILES, stride=8), :]
        si = sec_ref[1, part, pl.ds(i, TILES, stride=8), :]
        zr, zi = [], []
        for k in range(2):
            tr = twist_ref[0, k * TILES : (k + 1) * TILES]
            ti = twist_ref[1, k * TILES : (k + 1) * TILES]
            zr.append(sr * tr - si * ti)
            zi.append(si * tr + sr * ti)
        full = jnp.concatenate([jnp.concatenate(zr, 0), jnp.concatenate(zi, 0)], 1)
        top = full.astype(BF16)
        rest_ = (full - top.astype(F32)).astype(BF16)
        made = (
            lax.dot_general(high, top, contract, preferred_element_type=F32)
            + lax.dot_general(low, top, contract, preferred_element_type=F32)
            + lax.dot_general(high, rest_, contract, preferred_element_type=F32)
        )
        place_at = HALF - 1 - r if flip else r
        part, i = place_at // 8, place_at % 8
        out_ref[0, part, pl.ds(i, TILES, stride=8), :] = made[:TILES]
        out_ref[1, part, pl.ds(i, TILES, stride=8), :] = made[TILES:]


def tables(flip):
    shift = 1 if flip else 0
    k = np.arange(LANES)[:, None]
    n = np.arange(LANES)[None, :] + shift
    angle = -2 * np.pi * ((k * n) % G) / G
    twist = np.stack([np.cos(angle), np.sin(angle)]) / math.sqrt(G * K)
    t = np.arange(TILES)[:, None]
    angle = 2 * np.pi * ((t * n) % TILES) / TILES
    c, s = np.cos(angle), np.sin(angle)
    sign = -1.0 if flip else 1.0
    matrix = np.concatenate([np.concatenate([c, s], 1), sign * np.concatenate([-s, c], 1)], 0)
    high = matrix.astype(BF16)
    low = (matrix - high.astype(np.float64)).astype(BF16)
    return twist.astype(np.float32), np.stack([high, low])


def transform(rows, flip, earlier=None):
    vmem = pl.BlockSpec(memory_space=pltpu.VMEM)
    where = 1 if flip else 0
    args = list(map(jnp.asarray, tables(flip)))
    specs = [vmem, vmem, vmem]
    if earlier is not None:
        args.append(earlier)
        specs.append(pl.BlockSpec(memory_space=pl.ANY))
    return pl.pallas_call(
        functools.partial(transform_kernel, flip),
        grid=(1,),
        out_shape=jax.ShapeDtypeStruct((2, 4, 8 * TILES, LANES), F32),
        in_specs=specs,
        out_specs=pl.BlockSpec((2, 2, 8 * TILES, LANES), lambda i: (0, where, 0, 0)),
        scratch_shapes=[
            pltpu.VMEM((2, TILES, 8, LANES), F32),
            pltpu.VMEM((2, 2, 8 * TILES, LANES), F32),
        ],
        input_output_aliases={} if earlier is None else {3: 0},
        cost_estimate=pl.CostEstimate(flops=600_000_000, bytes_accessed=4_000_000, transcendentals=0),
        name="transform_mirror" if flip else "transform_own",
    )(rows, *args)


def shards(visibilities, coordinates, block_index, counts, col_offset):
    lists, firsts = spread_lists(
        visibilities[0], coordinates[0], block_index, counts, col_offset.reshape(2, 1, LANES)
    )
    own, low = place(firsts, lists)
    total = lax.axis_size("band") * lax.axis_size("wgrp")
    other = lax.ppermute(low, ("band", "wgrp"), [(i, total - 1 - i) for i in range(total)])
    out = transform(own, False)
    out = transform(other, True, out)
    out = out.reshape(2, 4, TILES, 8, LANES)
    return jnp.transpose(out, (0, 1, 3, 2, 4)).reshape(1, 2, S, G)


def solution(mesh):
    placed = (
        P("wgrp", "band", None),
        P("wgrp", "band", None),
        P("wgrp", "band"),
        P("wgrp", "band"),
        P("wgrp", "band"),
    )
    return jax.shard_map(
        shards, mesh=mesh, in_specs=placed, out_specs=P("wgrp", None, "band", None), check_vma=False
    )
```

```python
import math

import jax
import jax.numpy as jnp
import numpy as np
from jax import lax
from jax.experimental import pallas as pl
from jax.experimental.pallas import tpu as pltpu
from jax.sharding import PartitionSpec as P

S = 32
G = 8192
K = 256
CAP = 8
NBLK = 64
LANES = 128
TILES = G // LANES
MESH = pl.DeviceIdType.MESH
F32 = jnp.float32
BF16 = jnp.bfloat16


def fit(func, degree):
    nodes = 0.125 + 0.125 * np.cos(np.pi * (np.arange(400) + 0.5) / 400)
    series = np.polynomial.chebyshev.Chebyshev.fit(nodes, func(nodes), degree, domain=[0, 0.25])
    return [float(c) for c in series.convert(kind=np.polynomial.Polynomial).coef]


SIN_COEF = fit(lambda q: np.sin(2 * np.pi * np.sqrt(q)) / np.sqrt(q), 6)
COS_COEF = fit(lambda q: np.cos(2 * np.pi * np.sqrt(q)), 7)


def horner(coef, q):
    total = jnp.full_like(q, coef[-1])
    for c in coef[-2::-1]:
        total = total * q + c
    return total


def unit(cycles):
    frac = cycles - jnp.floor(cycles + 0.5)
    q = frac * frac
    return horner(COS_COEF, q), frac * horner(SIN_COEF, q)


def cmul(a, b):
    return a[0] * b[0] - a[1] * b[1], a[0] * b[1] + a[1] * b[0]


def spread(index_ref, counts_ref, vis_ref, coord_ref, offs_ref, recv_ref, roff_ref, *scratch):
    vf_ref, z_ref, sub_ref, send_ref, data_ref, table_ref, number_ref = scratch[:7]
    send_sem, recv_sem, osend_sem, orecv_sem, own_sem, dsend_sem, drecv_sem, number_sem = scratch[7:]
    band = lax.axis_index("band")
    plane = lax.axis_index("wgrp")
    z = band // 4
    x = band % 4
    twin = ((z + 4) % 8) * 4 + x

    def target(j):
        return ((z + j // 4) % 8) * 4 + (x + j % 4) % 4

    def device(half, e):
        return (e, plane + half * (7 - 2 * plane))

    barrier = pltpu.get_barrier_semaphore()

    def greet(j, carry):
        pl.semaphore_signal(barrier, inc=1, device_id=device(0, target(j)), device_id_type=MESH)
        pl.semaphore_signal(barrier, inc=1, device_id=device(1, target(j)), device_id_type=MESH)
        return carry

    lax.fori_loop(1, S, greet, 0)
    pl.semaphore_signal(barrier, inc=1, device_id=device(1, band), device_id_type=MESH)

    table_ref[0, 0:2] = index_ref[...]
    table_ref[0, 2, :, 0:S] = counts_ref[...]
    numbers = pltpu.make_async_copy(table_ref.at[0], number_ref.at[0], number_sem.at[0])
    numbers.start()
    sub_ref[:, NBLK] = jnp.zeros((2, 2 * S, LANES), BF16)
    sublane = lax.broadcasted_iota(jnp.int32, (8, K), 0)
    bits = [(sublane & bit) != 0 for bit in (1, 2, 4)]
    first = sublane == 0
    lane = lax.broadcasted_iota(jnp.int32, (2 * S, LANES), 1) // S

    def prepare(vis, coord):
        vf_ref[...] = vis.astype(F32)
        for axis in range(2):
            step = unit(coord[:, axis * K : (axis + 1) * K].astype(F32) * (1.0 / S))
            for which in range(5):
                z_ref[axis, which, 0] = step[0]
                z_ref[axis, which, 1] = step[1]
                if which < 4:
                    step = ((step[0] - step[1]) * (step[0] + step[1]), 2.0 * (step[0] * step[1]))

    def one_block(m):
        row = pl.ds(m, 1)

        def power(axis, which):
            return z_ref[axis, which, 0, row, :], z_ref[axis, which, 1, row, :]

        def exponents(axis):
            factors = []
            for which, bit in enumerate(bits):
                re, im = power(axis, which)
                factors.append((jnp.where(bit, re, 1.0), jnp.where(bit, im, 0.0)))
            base = cmul(cmul(factors[0], factors[1]), factors[2])
            z8 = power(axis, 3)
            z16 = power(axis, 4)
            rr, ii, ri, ir = z8[0] * base[0], z8[1] * base[1], z8[0] * base[1], z8[1] * base[0]
            low = (z16[0] * base[0] + z16[1] * base[1], z16[0] * base[1] - z16[1] * base[0])
            return (low, (rr + ii, ri - ir), base, (rr - ii, ri + ir)), z16

        def instead(part, other):
            return jnp.where(first, other[0], part[0]), jnp.where(first, other[1], part[1])

        parts, z16 = exponents(0)
        a, b = vf_ref[row, 0:K], vf_ref[row, K : 2 * K]
        plain, turned = [], []
        for i, (re, im) in enumerate(parts):
            ar, bi, ai, br = a * re, b * im, a * im, b * re
            plain.append((ar - bi, ai + br))
            if i == 0:
                re, im = instead((re, im), z16)
                ar, bi, ai, br = a * re, b * im, a * im, b * re
            turned.append((ar + bi, ai - br))
        right = jnp.concatenate(
            [
                jnp.concatenate([jnp.concatenate([c[i] for c in made], 0) for i in range(2)], 1).astype(BF16)
                for made in (plain, turned)
            ],
            0,
        )
        parts, z16 = exponents(1)

        def rows(pair):
            cos = jnp.concatenate([p[0] for p in pair], 0)
            sin = jnp.concatenate([p[1] for p in pair], 0)
            return (
                jnp.concatenate([cos, -sin], 1).astype(BF16),
                jnp.concatenate([sin, cos], 1).astype(BF16),
            )

        begin, end = rows(parts[:2]), rows(parts[2:])
        other = rows((instead(parts[0], z16), parts[1]))
        left = jnp.concatenate(
            [begin[0], end[0], begin[1], end[1], other[0], end[0], other[1], end[1]], 0
        )
        made = lax.dot_general(left, right, (((1,), (1,)), ((), ())), preferred_element_type=F32)
        sub_ref[0, m] = jnp.concatenate([made[: 2 * S, :S]] * 4, 1).astype(BF16)
        piece = pltpu.roll(jnp.concatenate([made[2 * S :, S:]] * 4, 1), LANES - 1, 1)
        sub_ref[1, m] = jnp.concatenate(
            [pltpu.roll(piece[:S], S - 1, 0), pltpu.roll(piece[S:], S - 1, 0)], 0
        ).astype(BF16)

    def blocks(begin, end):
        def some_blocks(i, carry):
            for j in range(4):
                one_block(i * 4 + j)
            return carry

        lax.fori_loop(begin // 4, end // 4, some_blocks, 0)

    def served(half, q):
        dz = 2 - half - (q // 4 + 3 - half) % 4
        return ((z + dz + 8) % 8) * 4 + (x + 3 - q % 4) % 4

    def expand(which, q):
        for half in range(2):
            e = served(half, q)
            d = e + half * (31 - 2 * e)
            live = number_ref[which, 2, 0, d]
            for group in range(2):
                idx = []
                for i in range(4):
                    slot = group * 4 + i
                    idx.append(
                        jnp.where(slot < live, number_ref[which, d // 16, 0, (d % 16) * CAP + slot], NBLK)
                    )
                value = sub_ref[half, idx[3]]
                for i in range(3):
                    value = jnp.where(lane == i, sub_ref[half, idx[i]], value)
                send_ref[which, half, q, group] = value

    def send(which, half, q):
        pltpu.make_async_remote_copy(
            src_ref=send_ref.at[which, half, q],
            dst_ref=recv_ref.at[half, twin if which else band],
            send_sem=send_sem.at[half],
            recv_sem=recv_sem.at[half],
            device_id=device(half, served(half, q)),
            device_id_type=MESH,
        ).start()

    def send_lists(which):
        expand(which, 0)

        def pass_on(q, carry):
            expand(which, q)
            send(which, 0, q - 1)
            send(which, 1, q - 1)
            return carry

        lax.fori_loop(1, 16, pass_on, 0)

    def inputs():
        pairs = ((vis_ref, data_ref.at[0]), (coord_ref, data_ref.at[1]), (table_ref.at[0], table_ref.at[1]))
        return [
            pltpu.make_async_remote_copy(
                src_ref=src,
                dst_ref=dst,
                send_sem=dsend_sem.at[i],
                recv_sem=drecv_sem.at[i],
                device_id=device(0, twin),
                device_id_type=MESH,
            )
            for i, (src, dst) in enumerate(pairs)
        ]

    def offsets(half, e):
        d = e + half * (31 - 2 * e)
        return pltpu.make_async_remote_copy(
            src_ref=offs_ref.at[d // 16],
            dst_ref=roff_ref.at[half, band],
            send_sem=osend_sem.at[half],
            recv_sem=orecv_sem.at[half],
            device_id=device(half, e),
            device_id_type=MESH,
        )

    prepare(vis_ref[...], coord_ref[...])
    blocks(0, NBLK // 2)
    pl.semaphore_wait(barrier, 2 * S - 1)
    for copy in inputs():
        copy.start()
    blocks(NBLK // 2, NBLK)
    numbers.wait()
    own_offs = pltpu.make_async_copy(offs_ref.at[band // 16], roff_ref.at[0, band], own_sem.at[1])
    own_offs.start()
    send_lists(0)
    send(0, 1, 15)
    own = pltpu.make_async_copy(send_ref.at[0, 0, 15], recv_ref.at[0, band], own_sem.at[0])
    own.start()
    for copy in inputs():
        copy.wait()
    numbers = pltpu.make_async_copy(table_ref.at[1], number_ref.at[1], number_sem.at[1])
    numbers.start()
    prepare(data_ref[0], data_ref[1])
    blocks(0, NBLK)
    numbers.wait()
    send_lists(1)
    send(1, 1, 15)
    twins = pltpu.make_async_copy(send_ref.at[1, 0, 15], recv_ref.at[0, twin], own_sem.at[2])
    twins.start()

    def tell(j, carry):
        offsets(0, target(j)).start()
        offsets(1, target(j)).start()
        return carry

    lax.fori_loop(1, S, tell, 0)
    offsets(1, band).start()
    own_offs.wait()
    own.wait()
    twins.wait()
    for half in range(2):
        for arrived, local, left_sem, come_sem in (
            (roff_ref, 1, osend_sem, orecv_sem),
            (recv_ref, 2, send_sem, recv_sem),
        ):
            everything = arrived.at[half, 0 : S if half else S - local]
            both = pltpu.make_async_remote_copy(
                src_ref=everything,
                dst_ref=everything,
                send_sem=left_sem.at[half],
                recv_sem=come_sem.at[half],
                device_id=device(1, band),
                device_id_type=MESH,
            )
            both.wait_send()
            both.wait_recv()


def spread_lists(vis, coord, index, counts, offsets):
    anywhere = pl.BlockSpec(memory_space=pl.ANY)
    vmem = pl.BlockSpec(memory_space=pltpu.VMEM)
    pair = pltpu.SemaphoreType.DMA((2,))
    three = pltpu.SemaphoreType.DMA((3,))
    return pl.pallas_call(
        spread,
        out_shape=(
            jax.ShapeDtypeStruct((2, S, 2, 2 * S, LANES), BF16),
            jax.ShapeDtypeStruct((2, S, 1, LANES), jnp.int32),
        ),
        in_specs=[vmem, vmem, vmem, vmem, anywhere],
        out_specs=(anywhere, anywhere),
        scratch_shapes=[
            pltpu.VMEM((NBLK, 2 * K), F32),
            pltpu.VMEM((2, 5, 2, NBLK, K), F32),
            pltpu.VMEM((2, NBLK + 1, 2 * S, LANES), BF16),
            pltpu.VMEM((2, 2, 16, 2, 2 * S, LANES), BF16),
            pltpu.VMEM((2, NBLK, 2 * K), BF16),
            pltpu.VMEM((2, 3, 1, LANES), jnp.int32),
            pltpu.SMEM((2, 3, 1, LANES), jnp.int32),
            pair,
            pair,
            pair,
            pair,
            three,
            three,
            three,
            pair,
        ],
        compiler_params=pltpu.CompilerParams(collective_id=0, has_side_effects=True),
        name="spread",
    )(index, counts, vis, coord, offsets)


def fft8(values):
    half = math.sqrt(0.5)

    def add(a, b):
        return a[0] + b[0], a[1] + b[1]

    def sub(a, b):
        return a[0] - b[0], a[1] - b[1]

    def turn(a):
        return a[1], -a[0]

    def fft4(v):
        s0, d0 = add(v[0], v[2]), sub(v[0], v[2])
        s1, d1 = add(v[1], v[3]), turn(sub(v[1], v[3]))
        return add(s0, s1), add(d0, d1), sub(s0, s1), sub(d0, d1)

    even = fft4(values[0::2])
    odd = fft4(values[1::2])
    o1 = ((odd[1][0] + odd[1][1]) * half, (odd[1][1] - odd[1][0]) * half)
    o2 = turn(odd[2])
    o3 = ((odd[3][1] - odd[3][0]) * half, (odd[3][0] + odd[3][1]) * -half)
    odd = (odd[0], o1, o2, o3)
    return [add(e, o) for e, o in zip(even, odd)] + [sub(e, o) for e, o in zip(even, odd)]


def finish_kernel(offs_ref, lists_ref, twist_ref, matrix_ref, out_ref, mid_ref, sec_ref, *slabs):
    part = pl.program_id(0)

    @pl.when(part == 0)
    def _():
        band = lax.axis_index("band")
        zero = jnp.zeros((8, LANES), F32)

        def clear(t, carry):
            for slab in slabs:
                slab[t] = jnp.zeros((2 * S, LANES), F32)
            return carry

        lax.fori_loop(0, TILES + 1, clear, 0)
        lane = lax.broadcasted_iota(jnp.int32, (8, LANES), 1)
        for half in range(2):
            base = ((31 - band if half else band) & 15) * CAP

            def place(i, carry, half=half, base=base):
                for group in range(2):
                    values = lists_ref[half, i, group].astype(F32)
                    for j, slab in enumerate(slabs):
                        start = offs_ref[half, i, 0, base + (group * 4 + j)]
                        if half:
                            start = G - S - start
                        tile = lax.shift_right_logical(start, 7)
                        first = start & (LANES - 1)
                        turned = pltpu.roll(values, (first - S * j) & (LANES - 1), 1)
                        inner = (lane >= first) & (lane < first + S)
                        outer = lane < first + (S - LANES)
                        for p in range(0, 2 * S, 8):
                            slab[tile, p : p + 8] += jnp.where(inner, turned[p : p + 8], zero)
                            slab[tile + 1, p : p + 8] += jnp.where(outer, turned[p : p + 8], zero)
                return carry

            lax.fori_loop(0, S, place, 0, unroll=2)

    def folded(t, row):
        at = pl.ds(pl.multiple_of(row, 8), 8)
        return (slabs[0][t, at] + slabs[1][t, at]) + (slabs[2][t, at] + slabs[3][t, at])

    for t2 in range(8):
        made = fft8([(folded(8 * t1 + t2, 8 * part), folded(8 * t1 + t2, 8 * part + S)) for t1 in range(8)])
        for q1 in range(8):
            re, im = made[q1]
            angle = -2 * math.pi * t2 * q1 / 64
            if t2 * q1:
                c, s = math.cos(angle), math.sin(angle)
                re, im = re * c - im * s, im * c + re * s
            mid_ref[0, q1 * 8 + t2] = re
            mid_ref[1, q1 * 8 + t2] = im
    for q1 in range(8):
        made = fft8([(mid_ref[0, q1 * 8 + t2], mid_ref[1, q1 * 8 + t2]) for t2 in range(8)])
        for q2 in range(8):
            at = (q1 + 8 * q2) * 8
            sec_ref[0, at : at + 8] = made[q2][0]
            sec_ref[1, at : at + 8] = made[q2][1]
    matrix = matrix_ref[...]
    for r in range(8):
        sr = sec_ref[0, pl.ds(r, TILES, stride=8), :]
        si = sec_ref[1, pl.ds(r, TILES, stride=8), :]
        zr, zi = [], []
        for k in range(2):
            tr = twist_ref[0, k * TILES : (k + 1) * TILES]
            ti = twist_ref[1, k * TILES : (k + 1) * TILES]
            zr.append(sr * tr - si * ti)
            zi.append(si * tr + sr * ti)
        full = jnp.concatenate([jnp.concatenate(zr, 0), jnp.concatenate(zi, 0)], 1).astype(BF16)
        made = lax.dot_general(matrix, full, (((1,), (1,)), ((), ())), preferred_element_type=F32)
        made = made[:LANES] + made[LANES:]
        out_ref[0, 0, pl.ds(r, TILES, stride=8), :] = made[:TILES]
        out_ref[1, 0, pl.ds(r, TILES, stride=8), :] = made[TILES:]


def tables():
    k = np.arange(LANES)[:, None]
    n = np.arange(LANES)[None, :]
    angle = -2 * np.pi * ((k * n) % G) / G
    twist = np.stack([np.cos(angle), np.sin(angle)]) / math.sqrt(G * K)
    t = np.arange(TILES)[:, None]
    angle = 2 * np.pi * ((t * n) % TILES) / TILES
    c, s = np.cos(angle), np.sin(angle)
    matrix = np.concatenate([np.concatenate([c, s], 1), np.concatenate([-s, c], 1)], 0)
    high = matrix.astype(BF16)
    low = (matrix - high.astype(np.float64)).astype(BF16)
    return twist.astype(np.float32), np.concatenate([high, low], 0)


def finish(offsets, lists):
    vmem = pl.BlockSpec(memory_space=pltpu.VMEM)
    return pl.pallas_call(
        finish_kernel,
        grid=(4,),
        out_shape=jax.ShapeDtypeStruct((2, 4, 8 * TILES, LANES), F32),
        in_specs=[pl.BlockSpec(memory_space=pltpu.SMEM), vmem, vmem, vmem],
        out_specs=pl.BlockSpec((2, 1, 8 * TILES, LANES), lambda i: (0, i, 0, 0)),
        scratch_shapes=[
            pltpu.VMEM((2, TILES, 8, LANES), F32),
            pltpu.VMEM((2, 8 * TILES, LANES), F32),
        ]
        + [pltpu.VMEM((TILES + 1, 2 * S, LANES), F32)] * 4,
        name="finish",
    )(offsets, lists, *map(jnp.asarray, tables()))


def shards(visibilities, coordinates, block_index, counts, col_offset):
    lists, firsts = spread_lists(
        visibilities[0],
        coordinates[0],
        block_index.reshape(2, 1, LANES),
        counts,
        col_offset.reshape(2, 1, LANES),
    )
    out = finish(firsts, lists)
    out = out.reshape(2, 4, TILES, 8, LANES)
    return jnp.transpose(out, (0, 1, 3, 2, 4)).reshape(1, 2, S, G)


def solution(mesh):
    placed = (
        P("wgrp", "band", None),
        P("wgrp", "band", None),
        P("wgrp", "band"),
        P("wgrp", "band"),
        P("wgrp", "band"),
    )
    return jax.shard_map(
        shards, mesh=mesh, in_specs=placed, out_specs=P("wgrp", None, "band", None), check_vma=False
    )
```

```python
import math

import jax
import jax.numpy as jnp
import numpy as np
from jax import lax
from jax.experimental import pallas as pl
from jax.experimental.pallas import tpu as pltpu
from jax.sharding import PartitionSpec as P

S = 32
G = 8192
K = 256
CAP = 8
NBLK = 64
LANES = 128
TILES = G // LANES
SLABS = 2
UNROLL = 8
MESH = pl.DeviceIdType.MESH
F32 = jnp.float32
BF16 = jnp.bfloat16


def fit(func, degree):
    nodes = 0.125 + 0.125 * np.cos(np.pi * (np.arange(400) + 0.5) / 400)
    series = np.polynomial.chebyshev.Chebyshev.fit(nodes, func(nodes), degree, domain=[0, 0.25])
    return [float(c) for c in series.convert(kind=np.polynomial.Polynomial).coef]


SIN_COEF = fit(lambda q: np.sin(2 * np.pi * np.sqrt(q)) / np.sqrt(q), 6)
COS_COEF = fit(lambda q: np.cos(2 * np.pi * np.sqrt(q)), 7)


def horner(coef, q):
    total = jnp.full_like(q, coef[-1])
    for c in coef[-2::-1]:
        total = total * q + c
    return total


def unit(cycles):
    frac = cycles - jnp.floor(cycles + 0.5)
    q = frac * frac
    return horner(COS_COEF, q), frac * horner(SIN_COEF, q)


def cmul(a, b):
    return a[0] * b[0] - a[1] * b[1], a[0] * b[1] + a[1] * b[0]


def spread(index_ref, counts_ref, vis_ref, coord_ref, offs_ref, recv_ref, roff_ref, *scratch):
    vf_ref, z_ref, sub_ref, send_ref, data_ref, table_ref, number_ref = scratch[:7]
    send_sem, recv_sem, osend_sem, orecv_sem, own_sem, dsend_sem, drecv_sem, number_sem = scratch[7:]
    band = lax.axis_index("band")
    plane = lax.axis_index("wgrp")
    z = band // 4
    x = band % 4
    twin = ((z + 4) % 8) * 4 + x

    def target(j):
        return ((z + j // 4) % 8) * 4 + (x + j % 4) % 4

    def device(half, e):
        return (e, plane + half * (7 - 2 * plane))

    barrier = pltpu.get_barrier_semaphore()

    def greet(j, carry):
        pl.semaphore_signal(barrier, inc=1, device_id=device(0, target(j)), device_id_type=MESH)
        pl.semaphore_signal(barrier, inc=1, device_id=device(1, target(j)), device_id_type=MESH)
        return carry

    lax.fori_loop(1, S, greet, 0)
    pl.semaphore_signal(barrier, inc=1, device_id=device(1, band), device_id_type=MESH)

    table_ref[0, 0:2] = index_ref[...]
    table_ref[0, 2, :, 0:S] = counts_ref[...]
    numbers = pltpu.make_async_copy(table_ref.at[0], number_ref.at[0], number_sem.at[0])
    numbers.start()
    sub_ref[:, NBLK] = jnp.zeros((2, 2 * S, LANES), BF16)
    sublane = lax.broadcasted_iota(jnp.int32, (8, K), 0)
    bits = [(sublane & bit) != 0 for bit in (1, 2, 4)]
    first = sublane == 0
    lane = lax.broadcasted_iota(jnp.int32, (2 * S, LANES), 1) // S

    def prepare(vis, coord):
        vf_ref[...] = vis.astype(F32)
        for axis in range(2):
            step = unit(coord[:, axis * K : (axis + 1) * K].astype(F32) * (1.0 / S))
            for which in range(5):
                z_ref[axis, which, 0] = step[0]
                z_ref[axis, which, 1] = step[1]
                if which < 4:
                    step = ((step[0] - step[1]) * (step[0] + step[1]), 2.0 * (step[0] * step[1]))

    def one_block(m):
        row = pl.ds(m, 1)

        def power(axis, which):
            return z_ref[axis, which, 0, row, :], z_ref[axis, which, 1, row, :]

        def exponents(axis):
            factors = []
            for which, bit in enumerate(bits):
                re, im = power(axis, which)
                factors.append((jnp.where(bit, re, 1.0), jnp.where(bit, im, 0.0)))
            base = cmul(cmul(factors[0], factors[1]), factors[2])
            z8 = power(axis, 3)
            z16 = power(axis, 4)
            rr, ii, ri, ir = z8[0] * base[0], z8[1] * base[1], z8[0] * base[1], z8[1] * base[0]
            low = (z16[0] * base[0] + z16[1] * base[1], z16[0] * base[1] - z16[1] * base[0])
            return (low, (rr + ii, ri - ir), base, (rr - ii, ri + ir)), z16

        def instead(part, other):
            return jnp.where(first, other[0], part[0]), jnp.where(first, other[1], part[1])

        parts, z16 = exponents(0)
        a, b = vf_ref[row, 0:K], vf_ref[row, K : 2 * K]
        plain, turned = [], []
        for i, (re, im) in enumerate(parts):
            ar, bi, ai, br = a * re, b * im, a * im, b * re
            plain.append((ar - bi, ai + br))
            if i == 0:
                re, im = instead((re, im), z16)
                ar, bi, ai, br = a * re, b * im, a * im, b * re
            turned.append((ar + bi, ai - br))
        right = jnp.concatenate(
            [
                jnp.concatenate([jnp.concatenate([c[i] for c in made], 0) for i in range(2)], 1).astype(BF16)
                for made in (plain, turned)
            ],
            0,
        )
        parts, z16 = exponents(1)

        def rows(pair):
            cos = jnp.concatenate([p[0] for p in pair], 0)
            sin = jnp.concatenate([p[1] for p in pair], 0)
            return (
                jnp.concatenate([cos, -sin], 1).astype(BF16),
                jnp.concatenate([sin, cos], 1).astype(BF16),
            )

        begin, end = rows(parts[:2]), rows(parts[2:])
        other = rows((instead(parts[0], z16), parts[1]))
        left = jnp.concatenate(
            [begin[0], end[0], begin[1], end[1], other[0], end[0], other[1], end[1]], 0
        )
        made = lax.dot_general(left, right, (((1,), (1,)), ((), ())), preferred_element_type=F32)
        sub_ref[0, m] = jnp.concatenate([made[: 2 * S, :S]] * 4, 1).astype(BF16)
        piece = pltpu.roll(jnp.concatenate([made[2 * S :, S:]] * 4, 1), LANES - 1, 1)
        sub_ref[1, m] = jnp.concatenate(
            [pltpu.roll(piece[:S], S - 1, 0), pltpu.roll(piece[S:], S - 1, 0)], 0
        ).astype(BF16)

    def blocks(begin, end):
        def some_blocks(i, carry):
            for j in range(4):
                one_block(i * 4 + j)
            return carry

        lax.fori_loop(begin // 4, end // 4, some_blocks, 0)

    def served(half, q):
        dz = 2 - half - (q // 4 + 3 - half) % 4
        return ((z + dz + 8) % 8) * 4 + (x + 3 - q % 4) % 4

    def expand(which, q):
        for half in range(2):
            e = served(half, q)
            d = e + half * (31 - 2 * e)
            live = number_ref[which, 2, 0, d]
            for group in range(2):
                idx = []
                for i in range(4):
                    slot = group * 4 + i
                    idx.append(
                        jnp.where(slot < live, number_ref[which, d // 16, 0, (d % 16) * CAP + slot], NBLK)
                    )
                value = sub_ref[half, idx[3]]
                for i in range(3):
                    value = jnp.where(lane == i, sub_ref[half, idx[i]], value)
                send_ref[which, half, q, group] = value

    def send(which, half, q):
        pltpu.make_async_remote_copy(
            src_ref=send_ref.at[which, half, q],
            dst_ref=recv_ref.at[half, twin if which else band],
            send_sem=send_sem.at[half],
            recv_sem=recv_sem.at[half],
            device_id=device(half, served(half, q)),
            device_id_type=MESH,
        ).start()

    def send_lists(which):
        expand(which, 0)

        def pass_on(q, carry):
            expand(which, q)
            send(which, 0, q - 1)
            send(which, 1, q - 1)
            return carry

        lax.fori_loop(1, 16, pass_on, 0)

    def inputs():
        pairs = ((vis_ref, data_ref.at[0]), (coord_ref, data_ref.at[1]), (table_ref.at[0], table_ref.at[1]))
        return [
            pltpu.make_async_remote_copy(
                src_ref=src,
                dst_ref=dst,
                send_sem=dsend_sem.at[i],
                recv_sem=drecv_sem.at[i],
                device_id=device(0, twin),
                device_id_type=MESH,
            )
            for i, (src, dst) in enumerate(pairs)
        ]

    def offsets(half, e):
        d = e + half * (31 - 2 * e)
        return pltpu.make_async_remote_copy(
            src_ref=offs_ref.at[d // 16],
            dst_ref=roff_ref.at[half, band],
            send_sem=osend_sem.at[half],
            recv_sem=orecv_sem.at[half],
            device_id=device(half, e),
            device_id_type=MESH,
        )

    prepare(vis_ref[...], coord_ref[...])
    blocks(0, NBLK // 2)
    pl.semaphore_wait(barrier, 2 * S - 1)
    for copy in inputs():
        copy.start()
    blocks(NBLK // 2, NBLK)
    numbers.wait()
    own_offs = pltpu.make_async_copy(offs_ref.at[band // 16], roff_ref.at[0, band], own_sem.at[1])
    own_offs.start()
    send_lists(0)
    send(0, 1, 15)
    own = pltpu.make_async_copy(send_ref.at[0, 0, 15], recv_ref.at[0, band], own_sem.at[0])
    own.start()

    def tell(j, carry):
        offsets(0, target(j)).start()
        offsets(1, target(j)).start()
        return carry

    lax.fori_loop(1, S, tell, 0)
    offsets(1, band).start()
    for copy in inputs():
        copy.wait()
    numbers = pltpu.make_async_copy(table_ref.at[1], number_ref.at[1], number_sem.at[1])
    numbers.start()
    prepare(data_ref[0], data_ref[1])
    blocks(0, NBLK)
    numbers.wait()
    send_lists(1)
    send(1, 1, 15)
    twins = pltpu.make_async_copy(send_ref.at[1, 0, 15], recv_ref.at[0, twin], own_sem.at[2])
    twins.start()

    own_offs.wait()
    own.wait()
    twins.wait()
    for half in range(2):
        for arrived, local, left_sem, come_sem in (
            (roff_ref, 1, osend_sem, orecv_sem),
            (recv_ref, 2, send_sem, recv_sem),
        ):
            everything = arrived.at[half, 0 : S if half else S - local]
            both = pltpu.make_async_remote_copy(
                src_ref=everything,
                dst_ref=everything,
                send_sem=left_sem.at[half],
                recv_sem=come_sem.at[half],
                device_id=device(1, band),
                device_id_type=MESH,
            )
            both.wait_send()
            both.wait_recv()


def spread_lists(vis, coord, index, counts, offsets):
    anywhere = pl.BlockSpec(memory_space=pl.ANY)
    vmem = pl.BlockSpec(memory_space=pltpu.VMEM)
    pair = pltpu.SemaphoreType.DMA((2,))
    three = pltpu.SemaphoreType.DMA((3,))
    return pl.pallas_call(
        spread,
        out_shape=(
            jax.ShapeDtypeStruct((2, S, 2, 2 * S, LANES), BF16),
            jax.ShapeDtypeStruct((2, S, 1, LANES), jnp.int32),
        ),
        in_specs=[vmem, vmem, vmem, vmem, anywhere],
        out_specs=(anywhere, anywhere),
        scratch_shapes=[
            pltpu.VMEM((NBLK, 2 * K), F32),
            pltpu.VMEM((2, 5, 2, NBLK, K), F32),
            pltpu.VMEM((2, NBLK + 1, 2 * S, LANES), BF16),
            pltpu.VMEM((2, 2, 16, 2, 2 * S, LANES), BF16),
            pltpu.VMEM((2, NBLK, 2 * K), BF16),
            pltpu.VMEM((2, 3, 1, LANES), jnp.int32),
            pltpu.SMEM((2, 3, 1, LANES), jnp.int32),
            pair,
            pair,
            pair,
            pair,
            three,
            three,
            three,
            pair,
        ],
        compiler_params=pltpu.CompilerParams(collective_id=0, has_side_effects=True),
        name="spread",
    )(index, counts, vis, coord, offsets)


def fft8(values):
    half = math.sqrt(0.5)

    def add(a, b):
        return a[0] + b[0], a[1] + b[1]

    def sub(a, b):
        return a[0] - b[0], a[1] - b[1]

    def turn(a):
        return a[1], -a[0]

    def fft4(v):
        s0, d0 = add(v[0], v[2]), sub(v[0], v[2])
        s1, d1 = add(v[1], v[3]), turn(sub(v[1], v[3]))
        return add(s0, s1), add(d0, d1), sub(s0, s1), sub(d0, d1)

    even = fft4(values[0::2])
    odd = fft4(values[1::2])
    o1 = ((odd[1][0] + odd[1][1]) * half, (odd[1][1] - odd[1][0]) * half)
    o2 = turn(odd[2])
    o3 = ((odd[3][1] - odd[3][0]) * half, (odd[3][0] + odd[3][1]) * -half)
    odd = (odd[0], o1, o2, o3)
    return [add(e, o) for e, o in zip(even, odd)] + [sub(e, o) for e, o in zip(even, odd)]


def finish_kernel(offs_ref, lists_any, twist_ref, matrix_ref, out_ref, mid_ref, sec_ref, lists_ref, sem, *slabs):
    part = pl.program_id(0)

    @pl.when(part == 0)
    def _():
        band = lax.axis_index("band")
        fetches = [
            pltpu.make_async_copy(lists_any.at[half], lists_ref.at[half], sem.at[half]) for half in range(2)
        ]
        for fetch in fetches:
            fetch.start()

        def clear(t, carry):
            for slab in slabs:
                slab[t] = jnp.zeros((2 * S, LANES), F32)
            return carry

        lax.fori_loop(0, TILES + 1, clear, 0)
        lane = lax.broadcasted_iota(jnp.int32, (8, LANES), 1)
        for half in range(2):
            fetches[half].wait()
            base = ((31 - band if half else band) & 15) * CAP

            def place(i, carry, half=half, base=base):
                for group in range(2):
                    values = lists_ref[half, i, group].astype(F32)
                    for j in range(4):
                        slab = slabs[j % len(slabs)]
                        start = offs_ref[half, i, 0, base + (group * 4 + j)]
                        if half:
                            start = G - S - start
                        tile = lax.shift_right_logical(start, 7)
                        first = start & (LANES - 1)
                        turned = pltpu.roll(values, (first - S * j) & (LANES - 1), 1)
                        inner = (lane >= first) & (lane < first + S)
                        outer = lane < first + (S - LANES)
                        for p in range(0, 2 * S, 8):
                            for at, mask in ((tile, inner), (tile + 1, outer)):
                                here = slab.at[at, p : p + 8]
                                pltpu.store(here, here[...] + turned[p : p + 8], mask=mask)
                return carry

            lax.fori_loop(0, S, place, 0, unroll=UNROLL)

    def folded(t, row):
        at = pl.ds(pl.multiple_of(row, 8), 8)
        total = slabs[0][t, at]
        for slab in slabs[1:]:
            total = total + slab[t, at]
        return total

    for t2 in range(8):
        made = fft8([(folded(8 * t1 + t2, 8 * part), folded(8 * t1 + t2, 8 * part + S)) for t1 in range(8)])
        for q1 in range(8):
            re, im = made[q1]
            angle = -2 * math.pi * t2 * q1 / 64
            if t2 * q1:
                c, s = math.cos(angle), math.sin(angle)
                re, im = re * c - im * s, im * c + re * s
            mid_ref[0, q1 * 8 + t2] = re
            mid_ref[1, q1 * 8 + t2] = im
    for q1 in range(8):
        made = fft8([(mid_ref[0, q1 * 8 + t2], mid_ref[1, q1 * 8 + t2]) for t2 in range(8)])
        for q2 in range(8):
            at = (q1 + 8 * q2) * 8
            sec_ref[0, at : at + 8] = made[q2][0]
            sec_ref[1, at : at + 8] = made[q2][1]
    matrix = matrix_ref[...]
    for r in range(8):
        sr = sec_ref[0, pl.ds(r, TILES, stride=8), :]
        si = sec_ref[1, pl.ds(r, TILES, stride=8), :]
        zr, zi = [], []
        for k in range(2):
            tr = twist_ref[0, k * TILES : (k + 1) * TILES]
            ti = twist_ref[1, k * TILES : (k + 1) * TILES]
            zr.append(sr * tr - si * ti)
            zi.append(si * tr + sr * ti)
        full = jnp.concatenate([jnp.concatenate(zr, 0), jnp.concatenate(zi, 0)], 1).astype(BF16)
        made = lax.dot_general(matrix, full, (((1,), (1,)), ((), ())), preferred_element_type=F32)
        made = made[:LANES] + made[LANES:]
        out_ref[0, 0, pl.ds(r, TILES, stride=8), :] = made[:TILES]
        out_ref[1, 0, pl.ds(r, TILES, stride=8), :] = made[TILES:]


def tables():
    k = np.arange(LANES)[:, None]
    n = np.arange(LANES)[None, :]
    angle = -2 * np.pi * ((k * n) % G) / G
    twist = np.stack([np.cos(angle), np.sin(angle)]) / math.sqrt(G * K)
    t = np.arange(TILES)[:, None]
    angle = 2 * np.pi * ((t * n) % TILES) / TILES
    c, s = np.cos(angle), np.sin(angle)
    matrix = np.concatenate([np.concatenate([c, s], 1), np.concatenate([-s, c], 1)], 0)
    high = matrix.astype(BF16)
    low = (matrix - high.astype(np.float64)).astype(BF16)
    return twist.astype(np.float32), np.concatenate([high, low], 0)


def finish(offsets, lists):
    vmem = pl.BlockSpec(memory_space=pltpu.VMEM)
    return pl.pallas_call(
        finish_kernel,
        grid=(4,),
        out_shape=jax.ShapeDtypeStruct((2, 4, 8 * TILES, LANES), F32),
        in_specs=[
            pl.BlockSpec(memory_space=pltpu.SMEM),
            pl.BlockSpec(memory_space=pl.ANY),
            vmem,
            vmem,
        ],
        out_specs=pl.BlockSpec((2, 1, 8 * TILES, LANES), lambda i: (0, i, 0, 0)),
        scratch_shapes=[
            pltpu.VMEM((2, TILES, 8, LANES), F32),
            pltpu.VMEM((2, 8 * TILES, LANES), F32),
            pltpu.VMEM((2, S, 2, 2 * S, LANES), BF16),
            pltpu.SemaphoreType.DMA((2,)),
        ]
        + [pltpu.VMEM((TILES + 1, 2 * S, LANES), F32)] * SLABS,
        name="finish",
    )(offsets, lists, *map(jnp.asarray, tables()))


def shards(visibilities, coordinates, block_index, counts, col_offset):
    lists, firsts = spread_lists(
        visibilities[0],
        coordinates[0],
        block_index.reshape(2, 1, LANES),
        counts,
        col_offset.reshape(2, 1, LANES),
    )
    out = finish(firsts, lists)
    out = out.reshape(2, 4, TILES, 8, LANES)
    return jnp.transpose(out, (0, 1, 3, 2, 4)).reshape(1, 2, S, G)


def solution(mesh):
    placed = (
        P("wgrp", "band", None),
        P("wgrp", "band", None),
        P("wgrp", "band"),
        P("wgrp", "band"),
        P("wgrp", "band"),
    )
    return jax.shard_map(
        shards, mesh=mesh, in_specs=placed, out_specs=P("wgrp", None, "band", None), check_vma=False
    )
```

```python
import math

import jax
import jax.numpy as jnp
import numpy as np
from jax import lax
from jax.experimental import pallas as pl
from jax.experimental.pallas import tpu as pltpu
from jax.sharding import PartitionSpec as P

S = 32
G = 8192
K = 256
CAP = 8
NBLK = 64
LANES = 128
TILES = G // LANES
OWN = 20
TURN = 8
SLABS = 2
UNROLL = 8
MESH = pl.DeviceIdType.MESH
F32 = jnp.float32
BF16 = jnp.bfloat16


def fit(func, degree):
    nodes = 0.125 + 0.125 * np.cos(np.pi * (np.arange(400) + 0.5) / 400)
    series = np.polynomial.chebyshev.Chebyshev.fit(nodes, func(nodes), degree, domain=[0, 0.25])
    return [float(c) for c in series.convert(kind=np.polynomial.Polynomial).coef]


SIN_COEF = fit(lambda q: np.sin(2 * np.pi * np.sqrt(q)) / np.sqrt(q), 6)
COS_COEF = fit(lambda q: np.cos(2 * np.pi * np.sqrt(q)), 7)


def horner(coef, q):
    total = jnp.full_like(q, coef[-1])
    for c in coef[-2::-1]:
        total = total * q + c
    return total


def unit(cycles):
    frac = cycles - jnp.floor(cycles + 0.5)
    q = frac * frac
    return horner(COS_COEF, q), frac * horner(SIN_COEF, q)


def cmul(a, b):
    return a[0] * b[0] - a[1] * b[1], a[0] * b[1] + a[1] * b[0]


def spread(index_ref, counts_ref, vis_ref, coord_ref, offs_ref, recv_ref, roff_ref, *scratch):
    vf_ref, z_ref, sub_ref, send_ref, data_ref, table_ref, number_ref = scratch[:7]
    send_sem, recv_sem, osend_sem, orecv_sem, own_sem, dsend_sem, drecv_sem, number_sem = scratch[7:]
    band = lax.axis_index("band")
    plane = lax.axis_index("wgrp")
    z = band // 4
    x = band % 4
    twin = ((z + 4) % 8) * 4 + x

    def target(j):
        return ((z + j // 4) % 8) * 4 + (x + j % 4) % 4

    def device(half, e):
        return (e, plane + half * (7 - 2 * plane))

    barrier = pltpu.get_barrier_semaphore()

    def greet(j, carry):
        pl.semaphore_signal(barrier, inc=1, device_id=device(0, target(j)), device_id_type=MESH)
        pl.semaphore_signal(barrier, inc=1, device_id=device(1, target(j)), device_id_type=MESH)
        return carry

    lax.fori_loop(1, S, greet, 0)
    pl.semaphore_signal(barrier, inc=1, device_id=device(1, band), device_id_type=MESH)

    table_ref[0, 0:2] = index_ref[...]
    table_ref[0, 2, :, 0:S] = counts_ref[...]
    numbers = pltpu.make_async_copy(table_ref.at[0], number_ref.at[0], number_sem.at[0])
    numbers.start()
    sub_ref[:, NBLK] = jnp.zeros((2, 2 * S, LANES), BF16)
    sublane = lax.broadcasted_iota(jnp.int32, (8, K), 0)
    bits = [(sublane & bit) != 0 for bit in (1, 2, 4)]
    first = sublane == 0
    lane = lax.broadcasted_iota(jnp.int32, (2 * S, LANES), 1) // S

    def prepare(vis, coord):
        vf_ref[...] = vis.astype(F32)
        for axis in range(2):
            step = unit(coord[:, axis * K : (axis + 1) * K].astype(F32) * (1.0 / S))
            for which in range(5):
                z_ref[axis, which, 0] = step[0]
                z_ref[axis, which, 1] = step[1]
                if which < 4:
                    step = ((step[0] - step[1]) * (step[0] + step[1]), 2.0 * (step[0] * step[1]))

    def one_block(m):
        row = pl.ds(m, 1)

        def power(axis, which):
            return z_ref[axis, which, 0, row, :], z_ref[axis, which, 1, row, :]

        def exponents(axis):
            factors = []
            for which, bit in enumerate(bits):
                re, im = power(axis, which)
                factors.append((jnp.where(bit, re, 1.0), jnp.where(bit, im, 0.0)))
            base = cmul(cmul(factors[0], factors[1]), factors[2])
            z8 = power(axis, 3)
            z16 = power(axis, 4)
            rr, ii, ri, ir = z8[0] * base[0], z8[1] * base[1], z8[0] * base[1], z8[1] * base[0]
            low = (z16[0] * base[0] + z16[1] * base[1], z16[0] * base[1] - z16[1] * base[0])
            return (low, (rr + ii, ri - ir), base, (rr - ii, ri + ir)), z16

        def instead(part, other):
            return jnp.where(first, other[0], part[0]), jnp.where(first, other[1], part[1])

        parts, z16 = exponents(0)
        a, b = vf_ref[row, 0:K], vf_ref[row, K : 2 * K]
        plain, turned = [], []
        for i, (re, im) in enumerate(parts):
            ar, bi, ai, br = a * re, b * im, a * im, b * re
            plain.append((ar - bi, ai + br))
            if i == 0:
                re, im = instead((re, im), z16)
                ar, bi, ai, br = a * re, b * im, a * im, b * re
            turned.append((ar + bi, ai - br))
        right = jnp.concatenate(
            [
                jnp.concatenate([jnp.concatenate([c[i] for c in made], 0) for i in range(2)], 1).astype(BF16)
                for made in (plain, turned)
            ],
            0,
        )
        parts, z16 = exponents(1)

        def rows(pair):
            cos = jnp.concatenate([p[0] for p in pair], 0)
            sin = jnp.concatenate([p[1] for p in pair], 0)
            return (
                jnp.concatenate([cos, -sin], 1).astype(BF16),
                jnp.concatenate([sin, cos], 1).astype(BF16),
            )

        begin, end = rows(parts[:2]), rows(parts[2:])
        other = rows((instead(parts[0], z16), parts[1]))
        left = jnp.concatenate(
            [begin[0], end[0], begin[1], end[1], other[0], end[0], other[1], end[1]], 0
        )
        made = lax.dot_general(left, right, (((1,), (1,)), ((), ())), preferred_element_type=F32)
        sub_ref[0, m] = jnp.concatenate([made[: 2 * S, :S]] * 4, 1).astype(BF16)
        piece = pltpu.roll(jnp.concatenate([made[2 * S :, S:]] * 4, 1), LANES - 1, 1)
        sub_ref[1, m] = jnp.concatenate(
            [pltpu.roll(piece[:S], S - 1, 0), pltpu.roll(piece[S:], S - 1, 0)], 0
        ).astype(BF16)

    def blocks(begin, end):
        def some_blocks(i, carry):
            for j in range(TURN):
                one_block(i * TURN + j)
            return carry

        lax.fori_loop(begin // TURN, end // TURN, some_blocks, 0)

    def served(which, half, q):
        k = q // 4 + 2 * which
        dz = (2 - k // 2) * (2 * (k % 2) - 1)
        return ((z + dz + 8) % 8) * 4 + (x + 3 - q % 4) % 4

    def expand(which, q):
        for half in range(2):
            e = served(which, half, q)
            d = e + half * (31 - 2 * e)
            live = number_ref[which, 2, 0, d]
            for group in range(2):
                idx = []
                for i in range(4):
                    slot = group * 4 + i
                    idx.append(
                        jnp.where(slot < live, number_ref[which, d // 16, 0, (d % 16) * CAP + slot], NBLK)
                    )
                value = sub_ref[half, idx[3]]
                for i in range(3):
                    value = jnp.where(lane == i, sub_ref[half, idx[i]], value)
                send_ref[half, OWN * which + q, group] = value

    def send(which, half, q):
        pltpu.make_async_remote_copy(
            src_ref=send_ref.at[half, OWN * which + q],
            dst_ref=recv_ref.at[half, twin if which else band],
            send_sem=send_sem.at[half],
            recv_sem=recv_sem.at[half],
            device_id=device(half, served(which, half, q)),
            device_id_type=MESH,
        ).start()

    def send_lists(which):
        expand(which, 0)

        def pass_on(q, carry):
            expand(which, q)
            send(which, 0, q - 1)
            send(which, 1, q - 1)
            return carry

        lax.fori_loop(1, S - OWN if which else OWN, pass_on, 0)

    def inputs():
        pairs = ((vis_ref, data_ref.at[0]), (coord_ref, data_ref.at[1]), (table_ref.at[0], table_ref.at[1]))
        return [
            pltpu.make_async_remote_copy(
                src_ref=src,
                dst_ref=dst,
                send_sem=dsend_sem.at[i],
                recv_sem=drecv_sem.at[i],
                device_id=device(0, twin),
                device_id_type=MESH,
            )
            for i, (src, dst) in enumerate(pairs)
        ]

    def offsets(half, e):
        d = e + half * (31 - 2 * e)
        return pltpu.make_async_remote_copy(
            src_ref=offs_ref.at[d // 16],
            dst_ref=roff_ref.at[half, band],
            send_sem=osend_sem.at[half],
            recv_sem=orecv_sem.at[half],
            device_id=device(half, e),
            device_id_type=MESH,
        )

    prepare(vis_ref[...], coord_ref[...])
    blocks(0, NBLK // 2)
    pl.semaphore_wait(barrier, 2 * S - 1)
    for copy in inputs():
        copy.start()
    blocks(NBLK // 2, NBLK)
    numbers.wait()
    own_offs = pltpu.make_async_copy(offs_ref.at[band // 16], roff_ref.at[0, band], own_sem.at[1])
    own_offs.start()
    send_lists(0)
    send(0, 1, OWN - 1)
    own = pltpu.make_async_copy(send_ref.at[0, OWN - 1], recv_ref.at[0, band], own_sem.at[0])
    own.start()

    def tell(j, carry):
        offsets(0, target(j)).start()
        offsets(1, target(j)).start()
        return carry

    lax.fori_loop(1, S, tell, 0)
    offsets(1, band).start()
    for copy in inputs():
        copy.wait()
    numbers = pltpu.make_async_copy(table_ref.at[1], number_ref.at[1], number_sem.at[1])
    numbers.start()
    prepare(data_ref[0], data_ref[1])
    blocks(0, NBLK)
    numbers.wait()
    send_lists(1)
    send(1, 1, S - OWN - 1)
    twins = pltpu.make_async_copy(send_ref.at[0, S - 1], recv_ref.at[0, twin], own_sem.at[2])
    twins.start()

    own_offs.wait()
    own.wait()
    twins.wait()
    for half in range(2):
        for arrived, local, left_sem, come_sem in (
            (roff_ref, 1, osend_sem, orecv_sem),
            (recv_ref, 2, send_sem, recv_sem),
        ):
            everything = arrived.at[half, 0 : S if half else S - local]
            both = pltpu.make_async_remote_copy(
                src_ref=everything,
                dst_ref=everything,
                send_sem=left_sem.at[half],
                recv_sem=come_sem.at[half],
                device_id=device(1, band),
                device_id_type=MESH,
            )
            both.wait_send()
            both.wait_recv()


def spread_lists(vis, coord, index, counts, offsets):
    anywhere = pl.BlockSpec(memory_space=pl.ANY)
    vmem = pl.BlockSpec(memory_space=pltpu.VMEM)
    pair = pltpu.SemaphoreType.DMA((2,))
    three = pltpu.SemaphoreType.DMA((3,))
    return pl.pallas_call(
        spread,
        out_shape=(
            jax.ShapeDtypeStruct((2, S, 2, 2 * S, LANES), BF16),
            jax.ShapeDtypeStruct((2, S, 1, LANES), jnp.int32),
        ),
        in_specs=[vmem, vmem, vmem, vmem, anywhere],
        out_specs=(anywhere, anywhere),
        scratch_shapes=[
            pltpu.VMEM((NBLK, 2 * K), F32),
            pltpu.VMEM((2, 5, 2, NBLK, K), F32),
            pltpu.VMEM((2, NBLK + 1, 2 * S, LANES), BF16),
            pltpu.VMEM((2, S, 2, 2 * S, LANES), BF16),
            pltpu.VMEM((2, NBLK, 2 * K), BF16),
            pltpu.VMEM((2, 3, 1, LANES), jnp.int32),
            pltpu.SMEM((2, 3, 1, LANES), jnp.int32),
            pair,
            pair,
            pair,
            pair,
            three,
            three,
            three,
            pair,
        ],
        compiler_params=pltpu.CompilerParams(collective_id=0, has_side_effects=True),
        name="spread",
    )(index, counts, vis, coord, offsets)


def fft8(values):
    half = math.sqrt(0.5)

    def add(a, b):
        return a[0] + b[0], a[1] + b[1]

    def sub(a, b):
        return a[0] - b[0], a[1] - b[1]

    def turn(a):
        return a[1], -a[0]

    def fft4(v):
        s0, d0 = add(v[0], v[2]), sub(v[0], v[2])
        s1, d1 = add(v[1], v[3]), turn(sub(v[1], v[3]))
        return add(s0, s1), add(d0, d1), sub(s0, s1), sub(d0, d1)

    even = fft4(values[0::2])
    odd = fft4(values[1::2])
    o1 = ((odd[1][0] + odd[1][1]) * half, (odd[1][1] - odd[1][0]) * half)
    o2 = turn(odd[2])
    o3 = ((odd[3][1] - odd[3][0]) * half, (odd[3][0] + odd[3][1]) * -half)
    odd = (odd[0], o1, o2, o3)
    return [add(e, o) for e, o in zip(even, odd)] + [sub(e, o) for e, o in zip(even, odd)]


def finish_kernel(offs_ref, lists_any, twist_ref, matrix_ref, out_ref, mid_ref, sec_ref, lists_ref, sem, *slabs):
    part = pl.program_id(0)

    @pl.when(part == 0)
    def _():
        band = lax.axis_index("band")
        fetches = [
            pltpu.make_async_copy(lists_any.at[half], lists_ref.at[half], sem.at[half]) for half in range(2)
        ]
        for fetch in fetches:
            fetch.start()

        def clear(t, carry):
            for slab in slabs:
                slab[t] = jnp.zeros((2 * S, LANES), F32)
            return carry

        lax.fori_loop(0, TILES + 1, clear, 0)
        lane = lax.broadcasted_iota(jnp.int32, (8, LANES), 1)
        for half in range(2):
            fetches[half].wait()
            base = ((31 - band if half else band) & 15) * CAP

            def place(i, carry, half=half, base=base):
                for group in range(2):
                    values = lists_ref[half, i, group].astype(F32)
                    for j in range(4):
                        slab = slabs[j % len(slabs)]
                        start = offs_ref[half, i, 0, base + (group * 4 + j)]
                        if half:
                            start = G - S - start
                        tile = lax.shift_right_logical(start, 7)
                        first = start & (LANES - 1)
                        turned = pltpu.roll(values, (first - S * j) & (LANES - 1), 1)
                        inner = (lane >= first) & (lane < first + S)
                        outer = lane < first + (S - LANES)
                        for p in range(0, 2 * S, 8):
                            for at, mask in ((tile, inner), (tile + 1, outer)):
                                here = slab.at[at, p : p + 8]
                                pltpu.store(here, here[...] + turned[p : p + 8], mask=mask)
                return carry

            lax.fori_loop(0, S, place, 0, unroll=UNROLL)

    def folded(t, row):
        at = pl.ds(pl.multiple_of(row, 8), 8)
        total = slabs[0][t, at]
        for slab in slabs[1:]:
            total = total + slab[t, at]
        return total

    for t2 in range(8):
        made = fft8([(folded(8 * t1 + t2, 8 * part), folded(8 * t1 + t2, 8 * part + S)) for t1 in range(8)])
        for q1 in range(8):
            re, im = made[q1]
            angle = -2 * math.pi * t2 * q1 / 64
            if t2 * q1:
                c, s = math.cos(angle), math.sin(angle)
                re, im = re * c - im * s, im * c + re * s
            mid_ref[0, q1 * 8 + t2] = re
            mid_ref[1, q1 * 8 + t2] = im
    for q1 in range(8):
        made = fft8([(mid_ref[0, q1 * 8 + t2], mid_ref[1, q1 * 8 + t2]) for t2 in range(8)])
        for q2 in range(8):
            at = (q1 + 8 * q2) * 8
            sec_ref[0, at : at + 8] = made[q2][0]
            sec_ref[1, at : at + 8] = made[q2][1]
    matrix = matrix_ref[...]
    for r in range(8):
        sr = sec_ref[0, pl.ds(r, TILES, stride=8), :]
        si = sec_ref[1, pl.ds(r, TILES, stride=8), :]
        zr, zi = [], []
        for k in range(2):
            tr = twist_ref[0, k * TILES : (k + 1) * TILES]
            ti = twist_ref[1, k * TILES : (k + 1) * TILES]
            zr.append(sr * tr - si * ti)
            zi.append(si * tr + sr * ti)
        full = jnp.concatenate([jnp.concatenate(zr, 0), jnp.concatenate(zi, 0)], 1).astype(BF16)
        made = lax.dot_general(matrix, full, (((1,), (1,)), ((), ())), preferred_element_type=F32)
        made = made[:LANES] + made[LANES:]
        out_ref[0, 0, pl.ds(r, TILES, stride=8), :] = made[:TILES]
        out_ref[1, 0, pl.ds(r, TILES, stride=8), :] = made[TILES:]


def tables():
    k = np.arange(LANES)[:, None]
    n = np.arange(LANES)[None, :]
    angle = -2 * np.pi * ((k * n) % G) / G
    twist = np.stack([np.cos(angle), np.sin(angle)]) / math.sqrt(G * K)
    t = np.arange(TILES)[:, None]
    angle = 2 * np.pi * ((t * n) % TILES) / TILES
    c, s = np.cos(angle), np.sin(angle)
    matrix = np.concatenate([np.concatenate([c, s], 1), np.concatenate([-s, c], 1)], 0)
    high = matrix.astype(BF16)
    low = (matrix - high.astype(np.float64)).astype(BF16)
    return twist.astype(np.float32), np.concatenate([high, low], 0)


def finish(offsets, lists):
    vmem = pl.BlockSpec(memory_space=pltpu.VMEM)
    return pl.pallas_call(
        finish_kernel,
        grid=(4,),
        out_shape=jax.ShapeDtypeStruct((2, 4, 8 * TILES, LANES), F32),
        in_specs=[
            pl.BlockSpec(memory_space=pltpu.SMEM),
            pl.BlockSpec(memory_space=pl.ANY),
            vmem,
            vmem,
        ],
        out_specs=pl.BlockSpec((2, 1, 8 * TILES, LANES), lambda i: (0, i, 0, 0)),
        scratch_shapes=[
            pltpu.VMEM((2, TILES, 8, LANES), F32),
            pltpu.VMEM((2, 8 * TILES, LANES), F32),
            pltpu.VMEM((2, S, 2, 2 * S, LANES), BF16),
            pltpu.SemaphoreType.DMA((2,)),
        ]
        + [pltpu.VMEM((TILES + 1, 2 * S, LANES), F32)] * SLABS,
        name="finish",
    )(offsets, lists, *map(jnp.asarray, tables()))


def shards(visibilities, coordinates, block_index, counts, col_offset):
    lists, firsts = spread_lists(
        visibilities[0],
        coordinates[0],
        block_index.reshape(2, 1, LANES),
        counts,
        col_offset.reshape(2, 1, LANES),
    )
    out = finish(firsts, lists)
    out = out.reshape(2, 4, TILES, 8, LANES)
    return jnp.transpose(out, (0, 1, 3, 2, 4)).reshape(1, 2, S, G)


def solution(mesh):
    placed = (
        P("wgrp", "band", None),
        P("wgrp", "band", None),
        P("wgrp", "band"),
        P("wgrp", "band"),
        P("wgrp", "band"),
    )
    return jax.shard_map(
        shards, mesh=mesh, in_specs=placed, out_specs=P("wgrp", None, "band", None), check_vma=False
    )
```

```python
import math

import jax
import jax.numpy as jnp
import numpy as np
from jax import lax
from jax.experimental import pallas as pl
from jax.experimental.pallas import tpu as pltpu
from jax.sharding import PartitionSpec as P

S = 32
G = 8192
K = 256
CAP = 8
NBLK = 64
LANES = 128
TILES = G // LANES
OWN = 20
TURN = 8
SLABS = 2
UNROLL = 8
MESH = pl.DeviceIdType.MESH
F32 = jnp.float32
BF16 = jnp.bfloat16


def fit(func, degree):
    nodes = 0.125 + 0.125 * np.cos(np.pi * (np.arange(400) + 0.5) / 400)
    series = np.polynomial.chebyshev.Chebyshev.fit(nodes, func(nodes), degree, domain=[0, 0.25])
    return [float(c) for c in series.convert(kind=np.polynomial.Polynomial).coef]


SIN_COEF = fit(lambda q: np.sin(2 * np.pi * np.sqrt(q)) / np.sqrt(q), 6)
COS_COEF = fit(lambda q: np.cos(2 * np.pi * np.sqrt(q)), 7)


def horner(coef, q):
    total = jnp.full_like(q, coef[-1])
    for c in coef[-2::-1]:
        total = total * q + c
    return total


def unit(cycles):
    frac = cycles - jnp.floor(cycles + 0.5)
    q = frac * frac
    return horner(COS_COEF, q), frac * horner(SIN_COEF, q)


def cmul(a, b):
    return a[0] * b[0] - a[1] * b[1], a[0] * b[1] + a[1] * b[0]


def spread(index_ref, counts_ref, vis_ref, coord_ref, offs_ref, recv_ref, roff_ref, *scratch):
    vf_ref, z_ref, sub_ref, send_ref, data_ref, table_ref, number_ref = scratch[:7]
    send_sem, recv_sem, osend_sem, orecv_sem, own_sem, dsend_sem, drecv_sem, number_sem = scratch[7:]
    band = lax.axis_index("band")
    plane = lax.axis_index("wgrp")
    z = band // 4
    x = band % 4
    twin = ((z + 4) % 8) * 4 + x

    def target(j):
        return ((z + j // 4) % 8) * 4 + (x + j % 4) % 4

    def device(half, e):
        return (e, plane + half * (7 - 2 * plane))

    barrier = pltpu.get_barrier_semaphore()

    def greet(j, carry):
        pl.semaphore_signal(barrier, inc=1, device_id=device(0, target(j)), device_id_type=MESH)
        pl.semaphore_signal(barrier, inc=1, device_id=device(1, target(j)), device_id_type=MESH)
        return carry

    lax.fori_loop(1, S, greet, 0)
    pl.semaphore_signal(barrier, inc=1, device_id=device(1, band), device_id_type=MESH)

    table_ref[0, 0:2] = index_ref[...]
    table_ref[0, 2, :, 0:S] = counts_ref[...]
    numbers = pltpu.make_async_copy(table_ref.at[0], number_ref.at[0], number_sem.at[0])
    numbers.start()
    sub_ref[:, NBLK] = jnp.zeros((2, 2 * S, LANES), BF16)
    sublane = lax.broadcasted_iota(jnp.int32, (8, K), 0)
    bits = [(sublane & bit) != 0 for bit in (1, 2, 4)]
    first = sublane == 0
    lane = lax.broadcasted_iota(jnp.int32, (2 * S, LANES), 1) // S

    def prepare(vis, coord):
        vf_ref[...] = vis.astype(F32)
        for axis in range(2):
            step = unit(coord[:, axis * K : (axis + 1) * K].astype(F32) * (1.0 / S))
            for which in range(5):
                z_ref[axis, which, 0] = step[0]
                z_ref[axis, which, 1] = step[1]
                if which < 4:
                    step = ((step[0] - step[1]) * (step[0] + step[1]), 2.0 * (step[0] * step[1]))

    def one_block(m):
        row = pl.ds(m, 1)

        def power(axis, which):
            return z_ref[axis, which, 0, row, :], z_ref[axis, which, 1, row, :]

        def exponents(axis):
            factors = []
            for which, bit in enumerate(bits):
                re, im = power(axis, which)
                factors.append((jnp.where(bit, re, 1.0), jnp.where(bit, im, 0.0)))
            base = cmul(cmul(factors[0], factors[1]), factors[2])
            z8 = power(axis, 3)
            z16 = power(axis, 4)
            rr, ii, ri, ir = z8[0] * base[0], z8[1] * base[1], z8[0] * base[1], z8[1] * base[0]
            low = (z16[0] * base[0] + z16[1] * base[1], z16[0] * base[1] - z16[1] * base[0])
            return (low, (rr + ii, ri - ir), base, (rr - ii, ri + ir)), z16

        def instead(part, other):
            return jnp.where(first, other[0], part[0]), jnp.where(first, other[1], part[1])

        parts, z16 = exponents(0)
        a, b = vf_ref[row, 0:K], vf_ref[row, K : 2 * K]
        plain, turned = [], []
        for i, (re, im) in enumerate(parts):
            ar, bi, ai, br = a * re, b * im, a * im, b * re
            plain.append((ar - bi, ai + br))
            if i == 0:
                re, im = instead((re, im), z16)
                ar, bi, ai, br = a * re, b * im, a * im, b * re
            turned.append((ar + bi, ai - br))
        right = jnp.concatenate(
            [
                jnp.concatenate([jnp.concatenate([c[i] for c in made], 0) for i in range(2)], 1).astype(BF16)
                for made in (plain, turned)
            ],
            0,
        )
        parts, z16 = exponents(1)

        def rows(pair):
            cos = jnp.concatenate([p[0] for p in pair], 0)
            sin = jnp.concatenate([p[1] for p in pair], 0)
            return (
                jnp.concatenate([cos, -sin], 1).astype(BF16),
                jnp.concatenate([sin, cos], 1).astype(BF16),
            )

        begin, end = rows(parts[:2]), rows(parts[2:])
        other = rows((instead(parts[0], z16), parts[1]))
        left = jnp.concatenate(
            [begin[0], end[0], begin[1], end[1], other[0], end[0], other[1], end[1]], 0
        )
        made = lax.dot_general(left, right, (((1,), (1,)), ((), ())), preferred_element_type=F32)
        sub_ref[0, m] = jnp.concatenate([made[: 2 * S, :S]] * 4, 1).astype(BF16)
        piece = pltpu.roll(jnp.concatenate([made[2 * S :, S:]] * 4, 1), LANES - 1, 1)
        sub_ref[1, m] = jnp.concatenate(
            [pltpu.roll(piece[:S], S - 1, 0), pltpu.roll(piece[S:], S - 1, 0)], 0
        ).astype(BF16)

    def blocks(begin, end):
        def some_blocks(i, carry):
            for j in range(TURN):
                one_block(i * TURN + j)
            return carry

        lax.fori_loop(begin // TURN, end // TURN, some_blocks, 0)

    def served(which, half, q):
        k = q // 4 + 2 * which
        dz = (2 - k // 2) * (2 * (k % 2) - 1)
        return ((z + dz + 8) % 8) * 4 + (x + 3 - q % 4) % 4

    def expand(which, q):
        for half in range(2):
            e = served(which, half, q)
            d = e + half * (31 - 2 * e)
            live = number_ref[which, 2, 0, d]
            for group in range(2):
                idx = []
                for i in range(4):
                    slot = group * 4 + i
                    idx.append(
                        jnp.where(slot < live, number_ref[which, d // 16, 0, (d % 16) * CAP + slot], NBLK)
                    )
                value = sub_ref[half, idx[3]]
                for i in range(3):
                    value = jnp.where(lane == i, sub_ref[half, idx[i]], value)
                send_ref[half, OWN * which + q, group] = value

    def send(which, half, q):
        pltpu.make_async_remote_copy(
            src_ref=send_ref.at[half, OWN * which + q],
            dst_ref=recv_ref.at[half, twin if which else band],
            send_sem=send_sem.at[half],
            recv_sem=recv_sem.at[half],
            device_id=device(half, served(which, half, q)),
            device_id_type=MESH,
        ).start()

    def send_lists(which):
        expand(which, 0)

        def pass_on(q, carry):
            expand(which, q)
            send(which, 0, q - 1)
            send(which, 1, q - 1)
            return carry

        lax.fori_loop(1, S - OWN if which else OWN, pass_on, 0)

    def inputs():
        pairs = ((vis_ref, data_ref.at[0]), (coord_ref, data_ref.at[1]), (table_ref.at[0], table_ref.at[1]))
        return [
            pltpu.make_async_remote_copy(
                src_ref=src,
                dst_ref=dst,
                send_sem=dsend_sem.at[i],
                recv_sem=drecv_sem.at[i],
                device_id=device(0, twin),
                device_id_type=MESH,
            )
            for i, (src, dst) in enumerate(pairs)
        ]

    def offsets(half, e):
        d = e + half * (31 - 2 * e)
        return pltpu.make_async_remote_copy(
            src_ref=offs_ref.at[d // 16],
            dst_ref=roff_ref.at[half, band],
            send_sem=osend_sem.at[half],
            recv_sem=orecv_sem.at[half],
            device_id=device(half, e),
            device_id_type=MESH,
        )

    prepare(vis_ref[...], coord_ref[...])
    blocks(0, NBLK // 2)
    pl.semaphore_wait(barrier, 2 * S - 1)
    for copy in inputs():
        copy.start()
    blocks(NBLK // 2, NBLK)
    numbers.wait()
    own_offs = pltpu.make_async_copy(offs_ref.at[band // 16], roff_ref.at[0, band], own_sem.at[1])
    own_offs.start()
    send_lists(0)
    send(0, 1, OWN - 1)
    own = pltpu.make_async_copy(send_ref.at[0, OWN - 1], recv_ref.at[0, band], own_sem.at[0])
    own.start()

    def tell(j, carry):
        offsets(0, target(j)).start()
        offsets(1, target(j)).start()
        return carry

    lax.fori_loop(1, S, tell, 0)
    offsets(1, band).start()
    for copy in inputs():
        copy.wait()
    numbers = pltpu.make_async_copy(table_ref.at[1], number_ref.at[1], number_sem.at[1])
    numbers.start()
    prepare(data_ref[0], data_ref[1])
    blocks(0, NBLK)
    numbers.wait()
    send_lists(1)
    send(1, 1, S - OWN - 1)
    twins = pltpu.make_async_copy(send_ref.at[0, S - 1], recv_ref.at[0, twin], own_sem.at[2])
    twins.start()

    own_offs.wait()
    own.wait()
    twins.wait()
    for half in range(2):
        for arrived, local, left_sem, come_sem in (
            (roff_ref, 1, osend_sem, orecv_sem),
            (recv_ref, 2, send_sem, recv_sem),
        ):
            everything = arrived.at[half, 0 : S if half else S - local]
            both = pltpu.make_async_remote_copy(
                src_ref=everything,
                dst_ref=everything,
                send_sem=left_sem.at[half],
                recv_sem=come_sem.at[half],
                device_id=device(1, band),
                device_id_type=MESH,
            )
            both.wait_send()
            both.wait_recv()


def spread_lists(vis, coord, index, counts, offsets):
    anywhere = pl.BlockSpec(memory_space=pl.ANY)
    vmem = pl.BlockSpec(memory_space=pltpu.VMEM)
    pair = pltpu.SemaphoreType.DMA((2,))
    three = pltpu.SemaphoreType.DMA((3,))
    return pl.pallas_call(
        spread,
        out_shape=(
            jax.ShapeDtypeStruct((2, S, 2, 2 * S, LANES), BF16),
            jax.ShapeDtypeStruct((2, S, 1, LANES), jnp.int32),
        ),
        in_specs=[vmem, vmem, vmem, vmem, anywhere],
        out_specs=(anywhere, anywhere),
        scratch_shapes=[
            pltpu.VMEM((NBLK, 2 * K), F32),
            pltpu.VMEM((2, 5, 2, NBLK, K), F32),
            pltpu.VMEM((2, NBLK + 1, 2 * S, LANES), BF16),
            pltpu.VMEM((2, S, 2, 2 * S, LANES), BF16),
            pltpu.VMEM((2, NBLK, 2 * K), BF16),
            pltpu.VMEM((2, 3, 1, LANES), jnp.int32),
            pltpu.SMEM((2, 3, 1, LANES), jnp.int32),
            pair,
            pair,
            pair,
            pair,
            three,
            three,
            three,
            pair,
        ],
        compiler_params=pltpu.CompilerParams(collective_id=0, has_side_effects=True),
        name="spread",
    )(index, counts, vis, coord, offsets)


def fft8(values):
    half = math.sqrt(0.5)

    def add(a, b):
        return a[0] + b[0], a[1] + b[1]

    def sub(a, b):
        return a[0] - b[0], a[1] - b[1]

    def turn(a):
        return a[1], -a[0]

    def fft4(v):
        s0, d0 = add(v[0], v[2]), sub(v[0], v[2])
        s1, d1 = add(v[1], v[3]), turn(sub(v[1], v[3]))
        return add(s0, s1), add(d0, d1), sub(s0, s1), sub(d0, d1)

    even = fft4(values[0::2])
    odd = fft4(values[1::2])
    o1 = ((odd[1][0] + odd[1][1]) * half, (odd[1][1] - odd[1][0]) * half)
    o2 = turn(odd[2])
    o3 = ((odd[3][1] - odd[3][0]) * half, (odd[3][0] + odd[3][1]) * -half)
    odd = (odd[0], o1, o2, o3)
    return [add(e, o) for e, o in zip(even, odd)] + [sub(e, o) for e, o in zip(even, odd)]


def finish_kernel(offs_ref, lists_any, twist_ref, matrix_ref, out_any, out_ref, mid_ref, sec_ref, lists_ref, sem, *slabs):
    band = lax.axis_index("band")
    fetches = [
        pltpu.make_async_copy(lists_any.at[half], lists_ref.at[half], sem.at[half]) for half in range(2)
    ]
    for fetch in fetches:
        fetch.start()

    def clear(t, carry):
        for slab in slabs:
            slab[t] = jnp.zeros((2 * S, LANES), F32)
        return carry

    lax.fori_loop(0, TILES + 1, clear, 0)
    lane = lax.broadcasted_iota(jnp.int32, (8, LANES), 1)
    for half in range(2):
        fetches[half].wait()
        base = ((31 - band if half else band) & 15) * CAP

        def place(i, carry, half=half, base=base):
            for group in range(2):
                values = lists_ref[half, i, group].astype(F32)
                for j in range(4):
                    slab = slabs[j % len(slabs)]
                    start = offs_ref[half, i, 0, base + (group * 4 + j)]
                    if half:
                        start = G - S - start
                    tile = lax.shift_right_logical(start, 7)
                    first = start & (LANES - 1)
                    turned = pltpu.roll(values, (first - S * j) & (LANES - 1), 1)
                    inner = (lane >= first) & (lane < first + S)
                    outer = lane < first + (S - LANES)
                    for p in range(0, 2 * S, 8):
                        for at, mask in ((tile, inner), (tile + 1, outer)):
                            here = slab.at[at, p : p + 8]
                            pltpu.store(here, here[...] + turned[p : p + 8], mask=mask)
            return carry

        lax.fori_loop(0, S, place, 0, unroll=UNROLL)

    def folded(t, row):
        total = slabs[0][t, row : row + 8]
        for slab in slabs[1:]:
            total = total + slab[t, row : row + 8]
        return total

    def tiles(part):
        for t2 in range(8):
            made = fft8([(folded(8 * t1 + t2, 8 * part), folded(8 * t1 + t2, 8 * part + S)) for t1 in range(8)])
            for q1 in range(8):
                re, im = made[q1]
                angle = -2 * math.pi * t2 * q1 / 64
                if t2 * q1:
                    c, s = math.cos(angle), math.sin(angle)
                    re, im = re * c - im * s, im * c + re * s
                mid_ref[part, 0, q1 * 8 + t2] = re
                mid_ref[part, 1, q1 * 8 + t2] = im
        for q1 in range(8):
            made = fft8([(mid_ref[part, 0, q1 * 8 + t2], mid_ref[part, 1, q1 * 8 + t2]) for t2 in range(8)])
            for q2 in range(8):
                at = (q1 + 8 * q2) * 8
                sec_ref[part, 0, at : at + 8] = made[q2][0]
                sec_ref[part, 1, at : at + 8] = made[q2][1]

    matrix = matrix_ref[...]

    def rows(part):
        for r in range(8):
            at = pl.ds(r, TILES, stride=8)
            sr = sec_ref[part, 0, at, :]
            si = sec_ref[part, 1, at, :]
            zr, zi = [], []
            for k in range(2):
                tr = twist_ref[0, k * TILES : (k + 1) * TILES]
                ti = twist_ref[1, k * TILES : (k + 1) * TILES]
                zr.append(sr * tr - si * ti)
                zi.append(si * tr + sr * ti)
            full = jnp.concatenate([jnp.concatenate(zr, 0), jnp.concatenate(zi, 0)], 1).astype(BF16)
            made = lax.dot_general(matrix, full, (((1,), (1,)), ((), ())), preferred_element_type=F32)
            made = made[:LANES] + made[LANES:]
            out_ref[0, part, at, :] = made[:TILES]
            out_ref[1, part, at, :] = made[TILES:]

    leaves = []
    for part in range(4):
        tiles(part)
        if part:
            rows(part - 1)
            leaves.append(pltpu.make_async_copy(out_ref.at[:, part - 1], out_any.at[:, part - 1], sem.at[1 + part]))
            leaves[-1].start()
    rows(3)
    leaves.append(pltpu.make_async_copy(out_ref.at[:, 3], out_any.at[:, 3], sem.at[5]))
    leaves[-1].start()
    for leave in leaves:
        leave.wait()


def tables():
    k = np.arange(LANES)[:, None]
    n = np.arange(LANES)[None, :]
    angle = -2 * np.pi * ((k * n) % G) / G
    twist = np.stack([np.cos(angle), np.sin(angle)]) / math.sqrt(G * K)
    t = np.arange(TILES)[:, None]
    angle = 2 * np.pi * ((t * n) % TILES) / TILES
    c, s = np.cos(angle), np.sin(angle)
    matrix = np.concatenate([np.concatenate([c, s], 1), np.concatenate([-s, c], 1)], 0)
    high = matrix.astype(BF16)
    low = (matrix - high.astype(np.float64)).astype(BF16)
    return twist.astype(np.float32), np.concatenate([high, low], 0)


def finish(offsets, lists):
    vmem = pl.BlockSpec(memory_space=pltpu.VMEM)
    return pl.pallas_call(
        finish_kernel,
        out_shape=jax.ShapeDtypeStruct((2, 4, 8 * TILES, LANES), F32),
        in_specs=[
            pl.BlockSpec(memory_space=pltpu.SMEM),
            pl.BlockSpec(memory_space=pl.ANY),
            vmem,
            vmem,
        ],
        out_specs=pl.BlockSpec(memory_space=pl.ANY),
        scratch_shapes=[
            pltpu.VMEM((2, 4, 8 * TILES, LANES), F32),
            pltpu.VMEM((4, 2, TILES, 8, LANES), F32),
            pltpu.VMEM((4, 2, 8 * TILES, LANES), F32),
            pltpu.VMEM((2, S, 2, 2 * S, LANES), BF16),
            pltpu.SemaphoreType.DMA((6,)),
        ]
        + [pltpu.VMEM((TILES + 1, 2 * S, LANES), F32)] * SLABS,
        name="finish",
    )(offsets, lists, *map(jnp.asarray, tables()))


def shards(visibilities, coordinates, block_index, counts, col_offset):
    lists, firsts = spread_lists(
        visibilities[0],
        coordinates[0],
        block_index.reshape(2, 1, LANES),
        counts,
        col_offset.reshape(2, 1, LANES),
    )
    out = finish(firsts, lists)
    out = out.reshape(2, 4, TILES, 8, LANES)
    return jnp.transpose(out, (0, 1, 3, 2, 4)).reshape(1, 2, S, G)


def solution(mesh):
    placed = (
        P("wgrp", "band", None),
        P("wgrp", "band", None),
        P("wgrp", "band"),
        P("wgrp", "band"),
        P("wgrp", "band"),
    )
    return jax.shard_map(
        shards, mesh=mesh, in_specs=placed, out_specs=P("wgrp", None, "band", None), check_vma=False
    )
```

```python
import math

import jax
import jax.numpy as jnp
import numpy as np
from jax import lax
from jax.experimental import pallas as pl
from jax.experimental.pallas import tpu as pltpu
from jax.sharding import PartitionSpec as P

S = 32
G = 8192
K = 256
CAP = 8
NBLK = 64
LANES = 128
TILES = G // LANES
OWN = 20
TURN = 8
SLABS = 2
UNROLL = 8
MESH = pl.DeviceIdType.MESH
F32 = jnp.float32
BF16 = jnp.bfloat16


def fit(func, degree):
    nodes = 0.125 + 0.125 * np.cos(np.pi * (np.arange(400) + 0.5) / 400)
    series = np.polynomial.chebyshev.Chebyshev.fit(nodes, func(nodes), degree, domain=[0, 0.25])
    return [float(c) for c in series.convert(kind=np.polynomial.Polynomial).coef]


SIN_COEF = fit(lambda q: np.sin(2 * np.pi * np.sqrt(q)) / np.sqrt(q), 6)
COS_COEF = fit(lambda q: np.cos(2 * np.pi * np.sqrt(q)), 7)


def horner(coef, q):
    total = jnp.full_like(q, coef[-1])
    for c in coef[-2::-1]:
        total = total * q + c
    return total


def unit(cycles):
    frac = cycles - jnp.floor(cycles + 0.5)
    q = frac * frac
    return horner(COS_COEF, q), frac * horner(SIN_COEF, q)


def cmul(a, b):
    return a[0] * b[0] - a[1] * b[1], a[0] * b[1] + a[1] * b[0]


def spread(index_ref, counts_ref, vis_ref, coord_ref, offs_ref, recv_ref, roff_ref, *scratch):
    vf_ref, z_ref, sub_ref, send_ref, data_ref, table_ref, number_ref = scratch[:7]
    send_sem, recv_sem, osend_sem, orecv_sem, own_sem, dsend_sem, drecv_sem, number_sem = scratch[7:]
    band = lax.axis_index("band")
    plane = lax.axis_index("wgrp")
    z = band // 4
    x = band % 4
    twin = ((z + 4) % 8) * 4 + x

    def target(j):
        k = j // 4
        dz = 4 + ((k + 1) // 2) * (2 * (k % 2) - 1)
        return ((z + dz) % 8) * 4 + (x + 3 - j % 4) % 4

    def device(half, e):
        return (e, plane + half * (7 - 2 * plane))

    barrier = pltpu.get_barrier_semaphore()

    def greet(j, carry):
        pl.semaphore_signal(barrier, inc=1, device_id=device(0, target(j)), device_id_type=MESH)
        pl.semaphore_signal(barrier, inc=1, device_id=device(1, target(j)), device_id_type=MESH)
        return carry

    lax.fori_loop(0, S - 1, greet, 0)
    pl.semaphore_signal(barrier, inc=1, device_id=device(1, band), device_id_type=MESH)

    table_ref[0, 0:2] = index_ref[...]
    table_ref[0, 2, :, 0:S] = counts_ref[...]
    numbers = pltpu.make_async_copy(table_ref.at[0], number_ref.at[0], number_sem.at[0])
    numbers.start()
    sub_ref[:, NBLK] = jnp.zeros((2, 2 * S, LANES), BF16)
    sublane = lax.broadcasted_iota(jnp.int32, (8, K), 0)
    bits = [(sublane & bit) != 0 for bit in (1, 2, 4)]
    first = sublane == 0
    lane = lax.broadcasted_iota(jnp.int32, (2 * S, LANES), 1) // S

    def prepare(vis, coord):
        vf_ref[...] = vis.astype(F32)
        for axis in range(2):
            step = unit(coord[:, axis * K : (axis + 1) * K].astype(F32) * (1.0 / S))
            for which in range(5):
                z_ref[axis, which, 0] = step[0]
                z_ref[axis, which, 1] = step[1]
                if which < 4:
                    step = ((step[0] - step[1]) * (step[0] + step[1]), 2.0 * (step[0] * step[1]))

    def one_block(m):
        row = pl.ds(m, 1)

        def power(axis, which):
            return z_ref[axis, which, 0, row, :], z_ref[axis, which, 1, row, :]

        def exponents(axis):
            factors = []
            for which, bit in enumerate(bits):
                re, im = power(axis, which)
                factors.append((jnp.where(bit, re, 1.0), jnp.where(bit, im, 0.0)))
            base = cmul(cmul(factors[0], factors[1]), factors[2])
            z8 = power(axis, 3)
            z16 = power(axis, 4)
            rr, ii, ri, ir = z8[0] * base[0], z8[1] * base[1], z8[0] * base[1], z8[1] * base[0]
            low = (z16[0] * base[0] + z16[1] * base[1], z16[0] * base[1] - z16[1] * base[0])
            return (low, (rr + ii, ri - ir), base, (rr - ii, ri + ir)), z16

        def instead(part, other):
            return jnp.where(first, other[0], part[0]), jnp.where(first, other[1], part[1])

        parts, z16 = exponents(0)
        a, b = vf_ref[row, 0:K], vf_ref[row, K : 2 * K]
        plain, turned = [], []
        for i, (re, im) in enumerate(parts):
            ar, bi, ai, br = a * re, b * im, a * im, b * re
            plain.append((ar - bi, ai + br))
            if i == 0:
                re, im = instead((re, im), z16)
                ar, bi, ai, br = a * re, b * im, a * im, b * re
            turned.append((ar + bi, ai - br))
        right = jnp.concatenate(
            [
                jnp.concatenate([jnp.concatenate([c[i] for c in made], 0) for i in range(2)], 1).astype(BF16)
                for made in (plain, turned)
            ],
            0,
        )
        parts, z16 = exponents(1)

        def rows(pair):
            cos = jnp.concatenate([p[0] for p in pair], 0)
            sin = jnp.concatenate([p[1] for p in pair], 0)
            return (
                jnp.concatenate([cos, -sin], 1).astype(BF16),
                jnp.concatenate([sin, cos], 1).astype(BF16),
            )

        begin, end = rows(parts[:2]), rows(parts[2:])
        other = rows((instead(parts[0], z16), parts[1]))
        left = jnp.concatenate(
            [begin[0], end[0], begin[1], end[1], other[0], end[0], other[1], end[1]], 0
        )
        made = lax.dot_general(left, right, (((1,), (1,)), ((), ())), preferred_element_type=F32)
        sub_ref[0, m] = jnp.concatenate([made[: 2 * S, :S]] * 4, 1).astype(BF16)
        piece = pltpu.roll(jnp.concatenate([made[2 * S :, S:]] * 4, 1), LANES - 1, 1)
        sub_ref[1, m] = jnp.concatenate(
            [pltpu.roll(piece[:S], S - 1, 0), pltpu.roll(piece[S:], S - 1, 0)], 0
        ).astype(BF16)

    def blocks(begin, end):
        def some_blocks(i, carry):
            for j in range(TURN):
                one_block(i * TURN + j)
            return carry

        lax.fori_loop(begin // TURN, end // TURN, some_blocks, 0)

    def served(which, half, q):
        k = q // 4 + 2 * which
        dz = (2 - k // 2) * (2 * (k % 2) - 1)
        return ((z + dz + 8) % 8) * 4 + (x + 3 - q % 4) % 4

    def expand(which, q):
        for half in range(2):
            e = served(which, half, q)
            d = e + half * (31 - 2 * e)
            live = number_ref[which, 2, 0, d]
            for group in range(2):
                idx = []
                for i in range(4):
                    slot = group * 4 + i
                    idx.append(
                        jnp.where(slot < live, number_ref[which, d // 16, 0, (d % 16) * CAP + slot], NBLK)
                    )
                value = sub_ref[half, idx[3]]
                for i in range(3):
                    value = jnp.where(lane == i, sub_ref[half, idx[i]], value)
                send_ref[half, OWN * which + q, group] = value

    def send(which, half, q):
        pltpu.make_async_remote_copy(
            src_ref=send_ref.at[half, OWN * which + q],
            dst_ref=recv_ref.at[half, twin if which else band],
            send_sem=send_sem.at[half],
            recv_sem=recv_sem.at[half],
            device_id=device(half, served(which, half, q)),
            device_id_type=MESH,
        ).start()

    def send_lists(which):
        expand(which, 0)

        def pass_on(q, carry):
            expand(which, q)
            send(which, 0, q - 1)
            send(which, 1, q - 1)
            return carry

        lax.fori_loop(1, S - OWN if which else OWN, pass_on, 0)

    def inputs():
        pairs = ((vis_ref, data_ref.at[0]), (coord_ref, data_ref.at[1]), (table_ref.at[0], table_ref.at[1]))
        return [
            pltpu.make_async_remote_copy(
                src_ref=src,
                dst_ref=dst,
                send_sem=dsend_sem.at[i],
                recv_sem=drecv_sem.at[i],
                device_id=device(0, twin),
                device_id_type=MESH,
            )
            for i, (src, dst) in enumerate(pairs)
        ]

    def offsets(half, e):
        d = e + half * (31 - 2 * e)
        return pltpu.make_async_remote_copy(
            src_ref=offs_ref.at[d // 16],
            dst_ref=roff_ref.at[half, band],
            send_sem=osend_sem.at[half],
            recv_sem=orecv_sem.at[half],
            device_id=device(half, e),
            device_id_type=MESH,
        )

    prepare(vis_ref[...], coord_ref[...])
    blocks(0, NBLK // 2)
    pl.semaphore_wait(barrier, 2 * S - 1)
    for copy in inputs():
        copy.start()
    blocks(NBLK // 2, NBLK)
    numbers.wait()
    own_offs = pltpu.make_async_copy(offs_ref.at[band // 16], roff_ref.at[0, band], own_sem.at[1])
    own_offs.start()
    send_lists(0)
    send(0, 1, OWN - 1)
    own = pltpu.make_async_copy(send_ref.at[0, OWN - 1], recv_ref.at[0, band], own_sem.at[0])
    own.start()

    def tell(j, carry):
        offsets(0, target(j)).start()
        offsets(1, target(j)).start()
        return carry

    lax.fori_loop(0, S - 1, tell, 0)
    offsets(1, band).start()
    for copy in inputs():
        copy.wait()
    numbers = pltpu.make_async_copy(table_ref.at[1], number_ref.at[1], number_sem.at[1])
    numbers.start()
    prepare(data_ref[0], data_ref[1])
    blocks(0, NBLK)
    numbers.wait()
    send_lists(1)
    send(1, 1, S - OWN - 1)
    twins = pltpu.make_async_copy(send_ref.at[0, S - 1], recv_ref.at[0, twin], own_sem.at[2])
    twins.start()

    own_offs.wait()
    own.wait()
    twins.wait()
    for half in range(2):
        for arrived, local, left_sem, come_sem in (
            (roff_ref, 1, osend_sem, orecv_sem),
            (recv_ref, 2, send_sem, recv_sem),
        ):
            everything = arrived.at[half, 0 : S if half else S - local]
            both = pltpu.make_async_remote_copy(
                src_ref=everything,
                dst_ref=everything,
                send_sem=left_sem.at[half],
                recv_sem=come_sem.at[half],
                device_id=device(1, band),
                device_id_type=MESH,
            )
            both.wait_send()
            both.wait_recv()


def spread_lists(vis, coord, index, counts, offsets):
    anywhere = pl.BlockSpec(memory_space=pl.ANY)
    vmem = pl.BlockSpec(memory_space=pltpu.VMEM)
    pair = pltpu.SemaphoreType.DMA((2,))
    three = pltpu.SemaphoreType.DMA((3,))
    return pl.pallas_call(
        spread,
        out_shape=(
            jax.ShapeDtypeStruct((2, S, 2, 2 * S, LANES), BF16),
            jax.ShapeDtypeStruct((2, S, 1, LANES), jnp.int32),
        ),
        in_specs=[vmem, vmem, vmem, vmem, anywhere],
        out_specs=(anywhere, anywhere),
        scratch_shapes=[
            pltpu.VMEM((NBLK, 2 * K), F32),
            pltpu.VMEM((2, 5, 2, NBLK, K), F32),
            pltpu.VMEM((2, NBLK + 1, 2 * S, LANES), BF16),
            pltpu.VMEM((2, S, 2, 2 * S, LANES), BF16),
            pltpu.VMEM((2, NBLK, 2 * K), BF16),
            pltpu.VMEM((2, 3, 1, LANES), jnp.int32),
            pltpu.SMEM((2, 3, 1, LANES), jnp.int32),
            pair,
            pair,
            pair,
            pair,
            three,
            three,
            three,
            pair,
        ],
        compiler_params=pltpu.CompilerParams(collective_id=0, has_side_effects=True),
        name="spread",
    )(index, counts, vis, coord, offsets)


def fft8(values):
    half = math.sqrt(0.5)

    def add(a, b):
        return a[0] + b[0], a[1] + b[1]

    def sub(a, b):
        return a[0] - b[0], a[1] - b[1]

    def turn(a):
        return a[1], -a[0]

    def fft4(v):
        s0, d0 = add(v[0], v[2]), sub(v[0], v[2])
        s1, d1 = add(v[1], v[3]), turn(sub(v[1], v[3]))
        return add(s0, s1), add(d0, d1), sub(s0, s1), sub(d0, d1)

    even = fft4(values[0::2])
    odd = fft4(values[1::2])
    o1 = ((odd[1][0] + odd[1][1]) * half, (odd[1][1] - odd[1][0]) * half)
    o2 = turn(odd[2])
    o3 = ((odd[3][1] - odd[3][0]) * half, (odd[3][0] + odd[3][1]) * -half)
    odd = (odd[0], o1, o2, o3)
    return [add(e, o) for e, o in zip(even, odd)] + [sub(e, o) for e, o in zip(even, odd)]


def finish_kernel(offs_ref, lists_any, twist_ref, matrix_ref, out_any, out_ref, mid_ref, sec_ref, lists_ref, sem, *slabs):
    band = lax.axis_index("band")
    fetches = [
        pltpu.make_async_copy(lists_any.at[half], lists_ref.at[half], sem.at[half]) for half in range(2)
    ]
    for fetch in fetches:
        fetch.start()

    def clear(t, carry):
        for slab in slabs:
            slab[t] = jnp.zeros((2 * S, LANES), F32)
        return carry

    lax.fori_loop(0, TILES + 1, clear, 0, unroll=5)
    lane = lax.broadcasted_iota(jnp.int32, (8, LANES), 1)
    for half in range(2):
        fetches[half].wait()
        base = ((31 - band if half else band) & 15) * CAP

        def place(i, carry, half=half, base=base):
            for group in range(2):
                values = lists_ref[half, i, group].astype(F32)
                for j in range(4):
                    slab = slabs[j % len(slabs)]
                    start = offs_ref[half, i, 0, base + (group * 4 + j)]
                    if half:
                        start = G - S - start
                    tile = lax.shift_right_logical(start, 7)
                    first = start & (LANES - 1)
                    turned = pltpu.roll(values, (first - S * j) & (LANES - 1), 1)
                    inner = (lane >= first) & (lane < first + S)
                    outer = lane < first + (S - LANES)
                    for p in range(0, 2 * S, 8):
                        for at, mask in ((tile, inner), (tile + 1, outer)):
                            here = slab.at[at, p : p + 8]
                            pltpu.store(here, here[...] + turned[p : p + 8], mask=mask)
            return carry

        lax.fori_loop(0, S, place, 0, unroll=UNROLL)

    def folded(t, row):
        total = slabs[0][t, row : row + 8]
        for slab in slabs[1:]:
            total = total + slab[t, row : row + 8]
        return total

    def tiles(part):
        for t2 in range(8):
            made = fft8([(folded(8 * t1 + t2, 8 * part), folded(8 * t1 + t2, 8 * part + S)) for t1 in range(8)])
            for q1 in range(8):
                re, im = made[q1]
                angle = -2 * math.pi * t2 * q1 / 64
                if t2 * q1:
                    c, s = math.cos(angle), math.sin(angle)
                    re, im = re * c - im * s, im * c + re * s
                mid_ref[part, 0, q1 * 8 + t2] = re
                mid_ref[part, 1, q1 * 8 + t2] = im
        for q1 in range(8):
            made = fft8([(mid_ref[part, 0, q1 * 8 + t2], mid_ref[part, 1, q1 * 8 + t2]) for t2 in range(8)])
            for q2 in range(8):
                at = (q1 + 8 * q2) * 8
                sec_ref[part, 0, at : at + 8] = made[q2][0]
                sec_ref[part, 1, at : at + 8] = made[q2][1]

    matrix = matrix_ref[...]

    def rows(part):
        for r in range(8):
            at = pl.ds(r, TILES, stride=8)
            sr = sec_ref[part, 0, at, :]
            si = sec_ref[part, 1, at, :]
            zr, zi = [], []
            for k in range(2):
                tr = twist_ref[0, k * TILES : (k + 1) * TILES]
                ti = twist_ref[1, k * TILES : (k + 1) * TILES]
                zr.append(sr * tr - si * ti)
                zi.append(si * tr + sr * ti)
            full = jnp.concatenate([jnp.concatenate(zr, 0), jnp.concatenate(zi, 0)], 1).astype(BF16)
            made = lax.dot_general(matrix, full, (((1,), (1,)), ((), ())), preferred_element_type=F32)
            made = made[:LANES] + made[LANES:]
            out_ref[0, part, at, :] = made[:TILES]
            out_ref[1, part, at, :] = made[TILES:]

    leaves = []
    for part in range(4):
        tiles(part)
        if part:
            rows(part - 1)
            leaves.append(pltpu.make_async_copy(out_ref.at[:, part - 1], out_any.at[:, part - 1], sem.at[1 + part]))
            leaves[-1].start()
    rows(3)
    leaves.append(pltpu.make_async_copy(out_ref.at[:, 3], out_any.at[:, 3], sem.at[5]))
    leaves[-1].start()
    for leave in leaves:
        leave.wait()


def tables():
    k = np.arange(LANES)[:, None]
    n = np.arange(LANES)[None, :]
    angle = -2 * np.pi * ((k * n) % G) / G
    twist = np.stack([np.cos(angle), np.sin(angle)]) / math.sqrt(G * K)
    t = np.arange(TILES)[:, None]
    angle = 2 * np.pi * ((t * n) % TILES) / TILES
    c, s = np.cos(angle), np.sin(angle)
    matrix = np.concatenate([np.concatenate([c, s], 1), np.concatenate([-s, c], 1)], 0)
    high = matrix.astype(BF16)
    low = (matrix - high.astype(np.float64)).astype(BF16)
    return twist.astype(np.float32), np.concatenate([high, low], 0)


def finish(offsets, lists):
    vmem = pl.BlockSpec(memory_space=pltpu.VMEM)
    return pl.pallas_call(
        finish_kernel,
        out_shape=jax.ShapeDtypeStruct((2, 4, 8 * TILES, LANES), F32),
        in_specs=[
            pl.BlockSpec(memory_space=pltpu.SMEM),
            pl.BlockSpec(memory_space=pl.ANY),
            vmem,
            vmem,
        ],
        out_specs=pl.BlockSpec(memory_space=pl.ANY),
        scratch_shapes=[
            pltpu.VMEM((2, 4, 8 * TILES, LANES), F32),
            pltpu.VMEM((4, 2, TILES, 8, LANES), F32),
            pltpu.VMEM((4, 2, 8 * TILES, LANES), F32),
            pltpu.VMEM((2, S, 2, 2 * S, LANES), BF16),
            pltpu.SemaphoreType.DMA((6,)),
        ]
        + [pltpu.VMEM((TILES + 1, 2 * S, LANES), F32)] * SLABS,
        name="finish",
    )(offsets, lists, *map(jnp.asarray, tables()))


def shards(visibilities, coordinates, block_index, counts, col_offset):
    lists, firsts = spread_lists(
        visibilities[0],
        coordinates[0],
        block_index.reshape(2, 1, LANES),
        counts,
        col_offset.reshape(2, 1, LANES),
    )
    out = finish(firsts, lists)
    out = out.reshape(2, 4, TILES, 8, LANES)
    return jnp.transpose(out, (0, 1, 3, 2, 4)).reshape(1, 2, S, G)


def solution(mesh):
    placed = (
        P("wgrp", "band", None),
        P("wgrp", "band", None),
        P("wgrp", "band"),
        P("wgrp", "band"),
        P("wgrp", "band"),
    )
    return jax.shard_map(
        shards, mesh=mesh, in_specs=placed, out_specs=P("wgrp", None, "band", None), check_vma=False
    )
```
